32 devices in a mesh: grp: 2 (over x), seq: 16 (over z, y, core).
Axes of the slice: x: 2, y: 2, z: 4, core: 2. Of those that a mesh axis runs over, the one named last changes fastest.
Arguments:
- alignment: bfloat16 [128, 512, 768], P(('grp', 'seq')), parts along dimension 0, may hold values from -350 to 350
- depth_count: int32 [2], P('grp'), parts along dimension 0, may hold values from 16 to 64
- qkv_weight: bfloat16 [768, 2304], replicated, may hold values from -0.21650635 to 0.21650635
- pair_weight: bfloat16 [64, 12], replicated, may hold values from -1.75 to 1.75
- conv_weight: bfloat16 [4, 9, 64, 64], replicated, may hold values from -0.25 to 0.25
- head_weight: float32 [64], replicated, may hold values from -0.75 to 0.75
Outputs:
- row_mix: bfloat16 [128, 512, 768], P(('grp', 'seq')), parts along dimension 0
- contacts: float32 [1024, 512], P(('grp', 'seq')), parts along dimension 0
The draws below stay inside these ranges and needn't reach their ends.
There are 2 independent parts, one for each index of `grp`. The reference program is written for one: setup_inputs(seed, part) draws one part's arguments, and reference() takes and returns one part's arrays. A program takes and returns all parts, laid end to end along the dimension named above; an argument that names none is the same for every part. Nothing has to cross between parts.
Inputs may be any that keep to these rules, and one draw needn't show every extreme that they name: Sequences of alignment from index depth_count on are padding and take no part in the scores.
All inputs are finite; a program needn't handle non-finite values.
Results may differ from the reference program's by a relative error of at most 0.014.
Values may be sent and summed in bfloat16 or wider, within the bound.
No kernel may reach another device: no remote copies, remote signals or barrier semaphores. Data moves between devices by JAX's collectives and lax.ppermute only.
A program may use at most 192 MiB of HBM per device.

```python
import math
import jax
import jax.numpy as jnp
from jax import lax

D = 768
H = 12
E = 64
C = 64
BLOCKS = 2
L = 512
S = 64


def draw_alignment(key, part):
    pieces = jax.random.split(key, 1)
    return jnp.clip(jax.random.normal(pieces[0], (S, L, D), jnp.float32), -6.0, 6.0).astype(jnp.bfloat16)


def draw_qkv_weight(key, part):
    pieces = jax.random.split(key, 1)
    drawn = jnp.clip(jax.random.normal(pieces[0], (D, 3 * D), jnp.float32), -6.0, 6.0)
    return (drawn / math.sqrt(D)).astype(jnp.bfloat16)


def noise(key, extent, width, most, kind=jnp.bfloat16):
    array = jax.random.normal(key, extent, jnp.float32) * width
    return jnp.minimum(jnp.maximum(array, -most), most).astype(kind)


def setup_inputs(seed: int = 0, part: int = 0) -> dict:
    arg_keys = jax.random.split(jax.random.key(seed), 7)
    part_keys = jax.random.split(jax.random.fold_in(arg_keys[6], part), 7)
    alignment = draw_alignment(jax.random.fold_in(jax.random.fold_in(arg_keys[6], part), 71), part)
    depth_count = jax.random.randint(part_keys[1], (1,), S // 4, S + 1).astype(jnp.int32)
    qkv_weight = draw_qkv_weight(jax.random.fold_in(arg_keys[6], 71), part)
    pair_weight = noise(arg_keys[3], (C, H), H ** -0.5, 1.75)
    conv_weight = noise(arg_keys[4], (2 * BLOCKS, 9, C, C), (9 * C) ** -0.5, 0.25)
    head_weight = noise(arg_keys[5], (C,), C ** -0.5, 0.75, jnp.float32)
    return dict(alignment=alignment, depth_count=depth_count, qkv_weight=qkv_weight, pair_weight=pair_weight, conv_weight=conv_weight, head_weight=head_weight)


EPSILON = 1e-05

def layer_norm(values):
    values = values.astype(jnp.float32)
    average = lax.optimization_barrier(jnp.mean(values, axis=-1, keepdims=True))
    variance = lax.optimization_barrier(jnp.mean((values - average) ** 2, axis=-1, keepdims=True))
    return ((values - average) * lax.rsqrt(variance + EPSILON)).astype(jnp.bfloat16)

def dilated_full(source, kernel, dilation):
    padded = jnp.pad(source, ((0, 0), (dilation, dilation), (dilation, dilation)))
    summed = jnp.zeros(source.shape, jnp.float32)
    for tap_row in range(3):
        for tap_col in range(3):
            window = padded[:, tap_row * dilation:tap_row * dilation + L, tap_col * dilation:tap_col * dilation + L]
            summed = summed + jnp.einsum('oc,cij->oij', kernel[tap_row * 3 + tap_col].astype(jnp.float32), window.astype(jnp.float32))
    return summed

def reference(alignment, depth_count, qkv_weight, pair_weight, conv_weight, head_weight):
    normed = layer_norm(alignment)
    projected = jnp.dot(normed.reshape(S * L, D), qkv_weight, preferred_element_type=jnp.float32).astype(jnp.bfloat16)
    projected = projected.reshape(S, L, 3, H, E)
    queries = projected[:, :, 0]
    key_rows = projected[:, :, 1]
    value_rows = projected[:, :, 2]
    in_use = jnp.arange(S, dtype=jnp.int32) < depth_count[0]
    queries = jnp.where(in_use[:, None, None, None], queries, jnp.zeros_like(queries))
    score_scale = E ** (-0.5) / jnp.sqrt(depth_count[0].astype(jnp.float32))
    scores = jnp.einsum('sihe,sjhe->ihj', queries.astype(jnp.float32), key_rows.astype(jnp.float32)) * score_scale
    probabilities = jax.nn.softmax(scores, axis=-1).astype(jnp.bfloat16)
    prob_wide = probabilities.astype(jnp.float32)
    row_mix = jnp.einsum('ihj,sjhe->sihe', prob_wide, value_rows.astype(jnp.float32)).astype(jnp.bfloat16).reshape(S, L, D)
    pair_features = ((prob_wide.transpose(1, 0, 2) + prob_wide.transpose(1, 2, 0)) * (L * 0.5)).astype(jnp.bfloat16)
    hidden = jnp.einsum('ch,hij->cij', pair_weight.astype(jnp.float32), pair_features.astype(jnp.float32))
    for block_index in range(BLOCKS):
        dilation = block_index + 1
        hidden_round = hidden.astype(jnp.bfloat16)
        inner_act = jax.nn.relu(dilated_full(hidden_round, conv_weight[2 * block_index], dilation)).astype(jnp.bfloat16)
        hidden = hidden + dilated_full(inner_act, conv_weight[2 * block_index + 1], dilation)
    logits = jnp.einsum('c,cij->ij', head_weight, hidden, precision=lax.Precision.HIGHEST)
    contacts = 1.0 / (1.0 + jnp.exp(-logits))
    return (row_mix, contacts)
```

```python
import functools
import math

import jax
import jax.numpy as jnp
from jax import lax
from jax.experimental import pallas as pl
from jax.experimental.pallas import tpu as pltpu
from jax.sharding import PartitionSpec as P

EPSILON = 1e-05
LINK_SCALE = 2.0**-7


def grid_of(chips):
    width = 1
    while (2 * width) ** 2 <= chips:
        width *= 2
    return chips // width, width


def head_major(values, seqs, rows, size):
    out = []
    for head in range(values.shape[1] // size):
        pieces = [
            values[seq * rows : (seq + 1) * rows, head * size : (head + 1) * size]
            for seq in range(seqs)
        ]
        out.append(jnp.concatenate(pieces, axis=1))
    return out


def norm_send_kernel(half_ref, use_ref, x_ref, wq_ref, wk_ref, normed_ref, qk_ref):
    seqs, rows, width = x_ref.shape
    size = qk_ref.shape[3] // seqs
    values = x_ref[...].reshape(seqs * rows, width).astype(jnp.float32)
    average = jnp.mean(values, axis=-1, keepdims=True)
    centered = values - average
    variance = jnp.mean(centered * centered, axis=-1, keepdims=True)
    normed = (centered * lax.rsqrt(variance + EPSILON)).astype(jnp.bfloat16)
    normed_ref[...] = normed.reshape(seqs, rows, width)
    project(use_ref, normed, wq_ref, wk_ref, qk_ref, seqs, rows, size)


def own_kernel(half_ref, use_ref, normed_ref, wq_ref, wk_ref, qk_ref):
    seqs, rows, width = normed_ref.shape
    size = qk_ref.shape[3] // seqs
    normed = normed_ref[...].reshape(seqs * rows, width)
    project(use_ref, normed, wq_ref, wk_ref, qk_ref, seqs, rows, size)


def project(use_ref, normed, wq_ref, wk_ref, qk_ref, seqs, rows, size):
    q = jnp.dot(normed, wq_ref[...], preferred_element_type=jnp.float32).astype(jnp.bfloat16)
    for head, block in enumerate(head_major(q, seqs, rows, size)):
        lane = lax.broadcasted_iota(jnp.int32, block.shape, 1)
        qk_ref[0, head] = jnp.where(lane < use_ref[0] * size, block, jnp.zeros_like(block))
    k = jnp.dot(normed, wk_ref[...], preferred_element_type=jnp.float32).astype(jnp.bfloat16)
    for head, block in enumerate(head_major(k, seqs, rows, size)):
        qk_ref[1, head] = block


def value_kernel(normed_ref, w_ref, v_ref):
    seqs, rows, width = normed_ref.shape
    size = v_ref.shape[2] // seqs
    normed = normed_ref[...].reshape(seqs * rows, width)
    v = jnp.dot(normed, w_ref[...], preferred_element_type=jnp.float32).astype(jnp.bfloat16)
    for head, block in enumerate(head_major(v, seqs, rows, size)):
        v_ref[head] = block


def score_kernel(order_ref, scale_ref, own_ref, other_ref, s_ref):
    chips, _, rows, _ = s_ref.shape
    total = None
    for ref in (own_ref, other_ref):
        q = jnp.concatenate(
            [
                ref[0, 0, pl.ds(pl.multiple_of(order_ref[chip] * rows, rows), rows), :]
                for chip in range(chips)
            ],
            axis=0,
        )
        part = lax.dot_general(
            q, ref[1, 0], (((1,), (1,)), ((), ())), preferred_element_type=jnp.float32
        )
        total = part if total is None else total + part
    total = total * scale_ref[0]
    s_ref[...] = total.reshape(chips, 1, rows, total.shape[1])


def mix_kernel(p_ref, v_ref, o_ref):
    seqs = o_ref.shape[0]
    size = v_ref.shape[2] // seqs
    mixed = []
    for head in range(v_ref.shape[0]):
        probs = p_ref[0, :, head]
        probs = probs.reshape(probs.shape[0] * probs.shape[1], probs.shape[2])
        mixed.append(
            jnp.dot(probs, v_ref[head], preferred_element_type=jnp.float32).astype(jnp.bfloat16)
        )
    for seq in range(seqs):
        o_ref[seq] = jnp.concatenate(
            [block[:, seq * size : (seq + 1) * size] for block in mixed], axis=1
        )


def cost(flops, moved):
    return pl.CostEstimate(flops=int(flops), bytes_accessed=int(moved), transcendentals=0)


def projections(alignment, qkv_weight, half, use, head_count):
    seqs, residues, features = alignment.shape
    heads = head_count // 2
    size = features // head_count
    rows = 128 if residues % 128 == 0 else residues
    cols = heads * size
    steps = residues // rows
    bf16 = jnp.bfloat16
    x_spec = pl.BlockSpec((seqs, rows, features), lambda i, *_: (0, i, 0))
    qk_spec = pl.BlockSpec((2, heads, rows, seqs * size), lambda i, *_: (0, 0, i, 0))
    qk_shape = jax.ShapeDtypeStruct((2, heads, residues, seqs * size), bf16)
    params = pltpu.CompilerParams(vmem_limit_bytes=48 << 20)

    def weight_specs(pick):
        return [
            pl.BlockSpec((features, cols), lambda i, half, use: (0, pick(half[0]))),
            pl.BlockSpec((features, cols), lambda i, half, use: (0, 2 + pick(half[0]))),
        ]

    flops = 4 * seqs * residues * features * cols
    moved = 2 * (seqs * residues * features + 2 * features * cols + 2 * seqs * residues * cols)
    normed, sent = pl.pallas_call(
        norm_send_kernel,
        out_shape=(jax.ShapeDtypeStruct(alignment.shape, bf16), qk_shape),
        grid_spec=pltpu.PrefetchScalarGridSpec(
            num_scalar_prefetch=2,
            grid=(steps,),
            in_specs=[x_spec] + weight_specs(lambda half: 1 - half),
            out_specs=[x_spec, qk_spec],
        ),
        compiler_params=params,
        cost_estimate=cost(flops, moved + 2 * alignment.size),
        name="norm_send",
    )(half, use, alignment, qkv_weight, qkv_weight)
    own = pl.pallas_call(
        own_kernel,
        out_shape=qk_shape,
        grid_spec=pltpu.PrefetchScalarGridSpec(
            num_scalar_prefetch=2,
            grid=(steps,),
            in_specs=[x_spec] + weight_specs(lambda half: half),
            out_specs=qk_spec,
        ),
        compiler_params=params,
        cost_estimate=cost(flops, moved),
        name="own_project",
    )(half, use, normed, qkv_weight, qkv_weight)
    values = pl.pallas_call(
        value_kernel,
        out_shape=jax.ShapeDtypeStruct((head_count, residues, seqs * size), bf16),
        grid=(steps,),
        in_specs=[
            pl.BlockSpec((seqs, rows, features), lambda i: (0, i, 0)),
            pl.BlockSpec((features, features), lambda i: (0, 2)),
        ],
        out_specs=pl.BlockSpec((head_count, rows, seqs * size), lambda i: (0, i, 0)),
        compiler_params=params,
        cost_estimate=cost(flops, moved),
        name="value_project",
    )(normed, qkv_weight)
    return sent, own, values


def scores_of(own, other, order, scale, chips):
    _, heads, residues, inner = own.shape
    rows = residues // chips
    spec = pl.BlockSpec((2, 1, residues, inner), lambda h, *_: (0, h, 0, 0))
    return pl.pallas_call(
        score_kernel,
        out_shape=jax.ShapeDtypeStruct((chips, heads, rows, residues), jnp.float32),
        grid_spec=pltpu.PrefetchScalarGridSpec(
            num_scalar_prefetch=1,
            grid=(heads,),
            in_specs=[pl.BlockSpec(memory_space=pltpu.SMEM), spec, spec],
            out_specs=pl.BlockSpec((chips, 1, rows, residues), lambda h, *_: (0, h, 0, 0)),
        ),
        compiler_params=pltpu.CompilerParams(vmem_limit_bytes=32 << 20),
        cost_estimate=cost(4 * heads * residues * residues * inner, 4 * own.size + 4 * heads * residues**2),
        name="scores",
    )(order, scale, own, other)


def row_mix_of(probs, values, seqs, head_count):
    _, chips, heads, rows, residues = probs.shape
    inner = values.shape[2]
    size = inner // seqs
    pairs = heads // 2
    return pl.pallas_call(
        mix_kernel,
        out_shape=jax.ShapeDtypeStruct((seqs, residues, head_count * size), jnp.bfloat16),
        grid=(2 * pairs,),
        in_specs=[
            pl.BlockSpec((1, chips, 2, rows, residues), lambda g: (g // pairs, 0, g % pairs, 0, 0)),
            pl.BlockSpec((2, residues, inner), lambda g: (g, 0, 0)),
        ],
        out_specs=pl.BlockSpec((seqs, residues, 2 * size), lambda g: (0, 0, g)),
        compiler_params=pltpu.CompilerParams(vmem_limit_bytes=32 << 20),
        cost_estimate=cost(2 * probs.size * inner, 2 * (probs.size + 2 * values.size)),
        name="row_mix",
    )(probs, values)


class Links:
    def __init__(self):
        self.devices = lax.axis_size("seq")
        self.chips = self.devices // 2
        self.tall, self.wide = grid_of(self.chips)
        index = lax.axis_index("seq")
        self.index = index
        self.core = index % 2
        self.chip = index // 2
        self.z = self.chip // self.wide
        self.y = self.chip % self.wide

    def at(self, dz, dy):
        return (self.z + dz) % self.tall * self.wide + (self.y + dy) % self.wide

    def send(self, value, dz, dy, swap=False):
        pairs = []
        for source in range(self.devices):
            chip, core = divmod(source, 2)
            z, y = divmod(chip, self.wide)
            target = (z + dz) % self.tall * self.wide + (y + dy) % self.wide
            pairs.append((source, 2 * target + (1 - core if swap else core)))
        return lax.ppermute(value, "seq", pairs)


def reduce_scatter(links, scores):
    def piece(dz, dy):
        return scores[dz * links.wide + dy]

    half = jnp.float16
    far = sorted(range(links.tall), key=lambda dz: -min(dz, links.tall - dz))
    column = {}
    for dz in far:
        column[dz] = [
            links.send(piece(dz, dy).astype(half), 0, dy) for dy in range(1, links.wide)
        ]
    total = None
    for dz in far:
        summed = piece(dz, 0)
        for arrived in column[dz]:
            summed = summed + arrived.astype(jnp.float32)
        if dz:
            summed = links.send(summed.astype(half), dz, 0).astype(jnp.float32)
        total = summed if total is None else total + summed
    return total


def all_gather(links, own):
    gathered = jnp.zeros((2, links.chips) + own.shape, own.dtype)
    far = sorted(range(links.tall), key=lambda dz: -min(dz, links.tall - dz))
    zeros = (0,) * own.ndim
    pieces = []
    for dz in far:
        pieces.append((-dz, 0, links.send(own, dz, 0) if dz else own))
    pieces = pieces[-1:] + pieces[:-1]
    pieces += [
        (dz, -dy, links.send(value, 0, dy)) for dz, _, value in pieces for dy in range(1, links.wide)
    ]
    swapped = [links.send(value, 0, 0, swap=True) for _, _, value in pieces]
    for (dz, dy, value), other in zip(pieces, swapped):
        chip = links.at(dz, dy)
        gathered = lax.dynamic_update_slice(gathered, value[None, None], (links.core, chip) + zeros)
        gathered = lax.dynamic_update_slice(gathered, other[None, None], (1 - links.core, chip) + zeros)
    return gathered


def valid_rows(source, kernel, dilation):
    band_rows = source.shape[1] - 2 * dilation
    return lax.conv_general_dilated(
        source[None],
        kernel.reshape(3, 3, kernel.shape[1], kernel.shape[2]),
        (1, 1),
        ((0, 0), (dilation, dilation)),
        rhs_dilation=(dilation, dilation),
        dimension_numbers=("NCHW", "HWOI", "NCHW"),
        preferred_element_type=jnp.float32,
    )[0]


def contact_head(links, probs, pair_weight, conv_weight, head_weight):
    _, chips, heads, rows, residues = probs.shape
    probabilities = probs.transpose(1, 3, 0, 2, 4).reshape(residues, 2 * heads, residues)
    block_total = conv_weight.shape[0] // 2
    own_rows = residues // links.devices
    first_row = links.index * own_rows
    margin = block_total * (block_total + 1)
    band_rows = own_rows + 2 * margin
    widened = jnp.pad(probabilities, ((margin, margin), (0, 0), (margin, margin)))
    band_probs = lax.dynamic_slice_in_dim(widened, first_row, band_rows, 0)[
        :, :, margin : margin + residues
    ]
    band_cols = lax.dynamic_slice_in_dim(widened, first_row, band_rows, 2)[
        margin : margin + residues
    ]
    pair_features = (
        band_probs.astype(jnp.float32).transpose(1, 0, 2)
        + band_cols.astype(jnp.float32).transpose(1, 2, 0)
    ) * (residues * 0.5)
    pair_features = pair_features.astype(jnp.bfloat16)
    hidden = jnp.einsum(
        "ch,hrl->crl", pair_weight, pair_features, preferred_element_type=jnp.float32
    )
    row_ids = first_row - margin + jnp.arange(band_rows, dtype=jnp.int32)
    offset = 0
    for block_index in range(block_total):
        dilation = block_index + 1
        hidden_round = hidden.astype(jnp.bfloat16)
        inner_full = jax.nn.relu(valid_rows(hidden_round, conv_weight[2 * block_index], dilation))
        offset = offset + dilation
        inner_ids = row_ids[offset : band_rows - offset]
        inner_live = (inner_ids >= 0) & (inner_ids < residues)
        inner_act = jnp.where(inner_live[None, :, None], inner_full, 0.0).astype(jnp.bfloat16)
        offset = offset + dilation
        out_ids = row_ids[offset : band_rows - offset]
        out_live = (out_ids >= 0) & (out_ids < residues)
        updated = hidden[:, 2 * dilation : hidden.shape[1] - 2 * dilation] + valid_rows(
            inner_act, conv_weight[2 * block_index + 1], dilation
        )
        hidden = jnp.where(out_live[None, :, None], updated, 0.0)
    logits = jnp.einsum("c,crl->rl", head_weight, hidden, precision=lax.Precision.HIGHEST)
    return 1.0 / (1.0 + jnp.exp(-logits))


def local(alignment, depth_count, qkv_weight, pair_weight, conv_weight, head_weight):
    seqs, residues, features = alignment.shape
    head_count = pair_weight.shape[1]
    size = features // head_count
    links = Links()
    depth = depth_count[0]
    half = links.core.astype(jnp.int32).reshape(1)
    use = jnp.clip(depth - links.index * seqs, 0, seqs).astype(jnp.int32).reshape(1)
    sent, own, values = projections(alignment, qkv_weight, half, use, head_count)
    other = links.send(sent, 0, 0, swap=True)
    order = jnp.stack(
        [links.at(dz, dy) for dz in range(links.tall) for dy in range(links.wide)]
    ).astype(jnp.int32)
    scale = size**-0.5 / jnp.sqrt(depth.astype(jnp.float32)) * LINK_SCALE
    scores = scores_of(own, other, order, scale.reshape(1), links.chips)
    summed = reduce_scatter(links, scores) * (1.0 / LINK_SCALE)
    probabilities = jax.nn.softmax(summed, axis=-1).astype(jnp.bfloat16)
    gathered = all_gather(links, probabilities)
    row_mix = row_mix_of(gathered, values, seqs, head_count)
    contacts = contact_head(links, gathered, pair_weight, conv_weight, head_weight)
    return (row_mix, contacts)


def solution(mesh):
    return jax.shard_map(
        local,
        mesh=mesh,
        in_specs=(P(("grp", "seq"), None, None), P("grp"), P(), P(), P(), P()),
        out_specs=(P(("grp", "seq"), None, None), P(("grp", "seq"), None)),
        check_vma=False,
    )
```

```python
import functools
import math

import jax
import jax.numpy as jnp
from jax import lax
from jax.experimental import pallas as pl
from jax.experimental.pallas import tpu as pltpu
from jax.sharding import PartitionSpec as P

EPSILON = 1e-05
LINK_SCALE = 2.0**-7


def grid_of(chips):
    width = 1
    while (2 * width) ** 2 <= chips:
        width *= 2
    return chips // width, width


def head_major(values, seqs, rows, size):
    out = []
    for head in range(values.shape[1] // size):
        pieces = [
            values[seq * rows : (seq + 1) * rows, head * size : (head + 1) * size]
            for seq in range(seqs)
        ]
        out.append(jnp.concatenate(pieces, axis=1))
    return out


def norm_send_kernel(half_ref, use_ref, x_ref, wq_ref, wk_ref, normed_ref, qk_ref):
    seqs, rows, width = x_ref.shape
    size = qk_ref.shape[3] // seqs
    values = x_ref[...].reshape(seqs * rows, width).astype(jnp.float32)
    average = jnp.mean(values, axis=-1, keepdims=True)
    centered = values - average
    variance = jnp.mean(centered * centered, axis=-1, keepdims=True)
    normed = (centered * lax.rsqrt(variance + EPSILON)).astype(jnp.bfloat16)
    normed_ref[...] = normed.reshape(seqs, rows, width)
    project(use_ref, normed, wq_ref, wk_ref, qk_ref, seqs, rows, size)


def own_kernel(half_ref, use_ref, normed_ref, wq_ref, wk_ref, qk_ref):
    seqs, rows, width = normed_ref.shape
    size = qk_ref.shape[3] // seqs
    normed = normed_ref[...].reshape(seqs * rows, width)
    project(use_ref, normed, wq_ref, wk_ref, qk_ref, seqs, rows, size)


def project(use_ref, normed, wq_ref, wk_ref, qk_ref, seqs, rows, size):
    q = jnp.dot(normed, wq_ref[...], preferred_element_type=jnp.float32).astype(jnp.bfloat16)
    for head, block in enumerate(head_major(q, seqs, rows, size)):
        lane = lax.broadcasted_iota(jnp.int32, block.shape, 1)
        qk_ref[0, head] = jnp.where(lane < use_ref[0] * size, block, jnp.zeros_like(block))
    k = jnp.dot(normed, wk_ref[...], preferred_element_type=jnp.float32).astype(jnp.bfloat16)
    for head, block in enumerate(head_major(k, seqs, rows, size)):
        qk_ref[1, head] = block


def value_kernel(normed_ref, w_ref, v_ref):
    seqs, rows, width = normed_ref.shape
    size = v_ref.shape[2] // seqs
    normed = normed_ref[...].reshape(seqs * rows, width)
    v = jnp.dot(normed, w_ref[...], preferred_element_type=jnp.float32).astype(jnp.bfloat16)
    for head, block in enumerate(head_major(v, seqs, rows, size)):
        v_ref[head] = block


def score_kernel(order_ref, scale_ref, own_ref, other_ref, s_ref):
    chips, _, rows, _ = s_ref.shape
    total = None
    for ref in (own_ref, other_ref):
        q = jnp.concatenate(
            [
                ref[0, 0, pl.ds(pl.multiple_of(order_ref[chip] * rows, rows), rows), :]
                for chip in range(chips)
            ],
            axis=0,
        )
        part = lax.dot_general(
            q, ref[1, 0], (((1,), (1,)), ((), ())), preferred_element_type=jnp.float32
        )
        total = part if total is None else total + part
    total = total * scale_ref[0]
    s_ref[...] = total.reshape(chips, 1, rows, total.shape[1])


def mix_kernel(p_ref, v_ref, o_ref):
    seqs = o_ref.shape[0]
    size = v_ref.shape[2] // seqs
    mixed = []
    for head in range(v_ref.shape[0]):
        probs = p_ref[0, :, head]
        probs = probs.reshape(probs.shape[0] * probs.shape[1], probs.shape[2])
        mixed.append(
            jnp.dot(probs, v_ref[head], preferred_element_type=jnp.float32).astype(jnp.bfloat16)
        )
    for seq in range(seqs):
        o_ref[seq] = jnp.concatenate(
            [block[:, seq * size : (seq + 1) * size] for block in mixed], axis=1
        )


def cost(flops, moved):
    return pl.CostEstimate(flops=int(flops), bytes_accessed=int(moved), transcendentals=0)


def projections(alignment, qkv_weight, half, use, head_count):
    seqs, residues, features = alignment.shape
    heads = head_count // 2
    size = features // head_count
    rows = 128 if residues % 128 == 0 else residues
    cols = heads * size
    steps = residues // rows
    bf16 = jnp.bfloat16
    x_spec = pl.BlockSpec((seqs, rows, features), lambda i, *_: (0, i, 0))
    qk_spec = pl.BlockSpec((2, heads, rows, seqs * size), lambda i, *_: (0, 0, i, 0))
    qk_shape = jax.ShapeDtypeStruct((2, heads, residues, seqs * size), bf16)
    params = pltpu.CompilerParams(vmem_limit_bytes=48 << 20)

    def weight_specs(pick):
        return [
            pl.BlockSpec((features, cols), lambda i, half, use: (0, pick(half[0]))),
            pl.BlockSpec((features, cols), lambda i, half, use: (0, 2 + pick(half[0]))),
        ]

    flops = 4 * seqs * residues * features * cols
    moved = 2 * (seqs * residues * features + 2 * features * cols + 2 * seqs * residues * cols)
    normed, sent = pl.pallas_call(
        norm_send_kernel,
        out_shape=(jax.ShapeDtypeStruct(alignment.shape, bf16), qk_shape),
        grid_spec=pltpu.PrefetchScalarGridSpec(
            num_scalar_prefetch=2,
            grid=(steps,),
            in_specs=[x_spec] + weight_specs(lambda half: 1 - half),
            out_specs=[x_spec, qk_spec],
        ),
        compiler_params=params,
        cost_estimate=cost(flops, moved + 2 * alignment.size),
        name="norm_send",
    )(half, use, alignment, qkv_weight, qkv_weight)
    own = pl.pallas_call(
        own_kernel,
        out_shape=qk_shape,
        grid_spec=pltpu.PrefetchScalarGridSpec(
            num_scalar_prefetch=2,
            grid=(steps,),
            in_specs=[x_spec] + weight_specs(lambda half: half),
            out_specs=qk_spec,
        ),
        compiler_params=params,
        cost_estimate=cost(flops, moved),
        name="own_project",
    )(half, use, normed, qkv_weight, qkv_weight)
    values = pl.pallas_call(
        value_kernel,
        out_shape=jax.ShapeDtypeStruct((head_count, residues, seqs * size), bf16),
        grid=(steps,),
        in_specs=[
            pl.BlockSpec((seqs, rows, features), lambda i: (0, i, 0)),
            pl.BlockSpec((features, features), lambda i: (0, 2)),
        ],
        out_specs=pl.BlockSpec((head_count, rows, seqs * size), lambda i: (0, i, 0)),
        compiler_params=params,
        cost_estimate=cost(flops, moved),
        name="value_project",
    )(normed, qkv_weight)
    return sent, own, values


def scores_of(own, other, order, scale, chips):
    _, heads, residues, inner = own.shape
    rows = residues // chips
    spec = pl.BlockSpec((2, 1, residues, inner), lambda h, *_: (0, h, 0, 0))
    return pl.pallas_call(
        score_kernel,
        out_shape=jax.ShapeDtypeStruct((chips, heads, rows, residues), jnp.float32),
        grid_spec=pltpu.PrefetchScalarGridSpec(
            num_scalar_prefetch=1,
            grid=(heads,),
            in_specs=[pl.BlockSpec(memory_space=pltpu.SMEM), spec, spec],
            out_specs=pl.BlockSpec((chips, 1, rows, residues), lambda h, *_: (0, h, 0, 0)),
        ),
        compiler_params=pltpu.CompilerParams(vmem_limit_bytes=32 << 20),
        cost_estimate=cost(4 * heads * residues * residues * inner, 4 * own.size + 4 * heads * residues**2),
        name="scores",
    )(order, scale, own, other)


def row_mix_of(probs, values, seqs, head_count):
    _, chips, heads, rows, residues = probs.shape
    inner = values.shape[2]
    size = inner // seqs
    pairs = heads // 2
    return pl.pallas_call(
        mix_kernel,
        out_shape=jax.ShapeDtypeStruct((seqs, residues, head_count * size), jnp.bfloat16),
        grid=(2 * pairs,),
        in_specs=[
            pl.BlockSpec((1, chips, 2, rows, residues), lambda g: (g // pairs, 0, g % pairs, 0, 0)),
            pl.BlockSpec((2, residues, inner), lambda g: (g, 0, 0)),
        ],
        out_specs=pl.BlockSpec((seqs, residues, 2 * size), lambda g: (0, 0, g)),
        compiler_params=pltpu.CompilerParams(vmem_limit_bytes=32 << 20),
        cost_estimate=cost(2 * probs.size * inner, 2 * (probs.size + 2 * values.size)),
        name="row_mix",
    )(probs, values)


class Links:
    def __init__(self):
        self.devices = lax.axis_size("seq")
        self.chips = self.devices // 2
        self.tall, self.wide = grid_of(self.chips)
        index = lax.axis_index("seq")
        self.index = index
        self.core = index % 2
        self.chip = index // 2
        self.z = self.chip // self.wide
        self.y = self.chip % self.wide

    def at(self, dz, dy):
        return (self.z + dz) % self.tall * self.wide + (self.y + dy) % self.wide

    def send(self, value, dz, dy, swap=False):
        pairs = []
        for source in range(self.devices):
            chip, core = divmod(source, 2)
            z, y = divmod(chip, self.wide)
            target = (z + dz) % self.tall * self.wide + (y + dy) % self.wide
            pairs.append((source, 2 * target + (1 - core if swap else core)))
        return lax.ppermute(value, "seq", pairs)


def reduce_scatter(links, scores):
    def piece(dz, dy):
        return scores[dz * links.wide + dy]

    half = jnp.float16
    far = sorted(range(links.tall), key=lambda dz: -min(dz, links.tall - dz))
    column = {}
    for dz in far:
        column[dz] = [
            links.send(piece(dz, dy).astype(half), 0, dy) for dy in range(1, links.wide)
        ]
    total = None
    for dz in far:
        summed = piece(dz, 0)
        for arrived in column[dz]:
            summed = summed + arrived.astype(jnp.float32)
        if dz:
            summed = links.send(summed.astype(half), dz, 0).astype(jnp.float32)
        total = summed if total is None else total + summed
    return total


def all_gather(links, own):
    gathered = jnp.zeros((2, links.chips) + own.shape, own.dtype)
    far = sorted(range(links.tall), key=lambda dz: -min(dz, links.tall - dz))
    zeros = (0,) * own.ndim
    pieces = []
    for dz in far:
        pieces.append((-dz, 0, links.send(own, dz, 0) if dz else own))
    pieces = pieces[-1:] + pieces[:-1]
    pieces += [
        (dz, -dy, links.send(value, 0, dy)) for dz, _, value in pieces for dy in range(1, links.wide)
    ]
    swapped = [links.send(value, 0, 0, swap=True) for _, _, value in pieces]
    for (dz, dy, value), other in zip(pieces, swapped):
        chip = links.at(dz, dy)
        gathered = lax.dynamic_update_slice(gathered, value[None, None], (links.core, chip) + zeros)
        gathered = lax.dynamic_update_slice(gathered, other[None, None], (1 - links.core, chip) + zeros)
    return gathered


ROWS = 4
REACH = {1: (0, 1, 2, 3, 4, -1), 2: (0, 1, 2, 3, -2, -1, 4, 5)}


def taps_kernel(w_ref, near_ref, far_ref):
    size = w_ref.shape[1]
    zero = jnp.zeros((size, size), w_ref.dtype)
    for dilation, out_ref in ((1, near_ref), (2, far_ref)):
        for which in range(2):
            base = 9 * (2 * (dilation - 1) + which)
            for col in range(3):
                for slot, row in enumerate(REACH[dilation]):
                    pieces = []
                    for out_row in range(ROWS):
                        step, rest = divmod(row - out_row, dilation)
                        live = rest == 0 and -1 <= step <= 1
                        pieces.append(w_ref[base + 3 * (step + 1) + col] if live else zero)
                    out_ref[which, col, slot * size : (slot + 1) * size, :] = jnp.concatenate(
                        pieces, axis=1
                    )


def contact_kernel(
    row_ref, pf_ref, pair_ref, near_ref, far_ref, head_ref, o_ref, u_ref, v_ref, hid_ref
):
    blocks, _, residues = pf_ref.shape
    lanes = pair_ref.shape[1]
    size = lanes // ROWS
    half = lanes // 2
    bf16 = jnp.bfloat16
    position = lax.broadcasted_iota(jnp.int32, (residues, lanes), 0)
    lane_row = lax.broadcasted_iota(jnp.int32, (1, lanes), 1) // size

    def masked(m, values):
        row = row_ref[0] + ROWS * (m - 2) + lane_row
        return jnp.where((row >= 0) & (row < residues), values, 0.0)

    def spread(ref, m, values, dilation):
        ref[1, m] = values.astype(bf16)
        left = jnp.where(position >= dilation, pltpu.roll(values, dilation, 0), 0.0)
        ref[0, m] = left.astype(bf16)
        right = jnp.where(
            position < residues - dilation, pltpu.roll(values, residues - dilation, 0), 0.0
        )
        ref[2, m] = right.astype(bf16)

    def conv(ref, m, w_ref, which, dilation):
        before = jnp.maximum(m - 1, 0)
        after = jnp.minimum(m + 1, blocks - 1)
        total = None
        for col in range(3):
            low = ref[col, before, :, half:]
            high = ref[col, after, :, :half]
            if dilation == 1:
                lane = lax.broadcasted_iota(jnp.int32, low.shape, 1)
                edge = [jnp.where(lane < size, high, low)]
            else:
                edge = [low, high]
            window = jnp.concatenate([ref[col, m]] + edge, axis=1)
            part = jnp.dot(window, w_ref[which, col], preferred_element_type=jnp.float32)
            total = part if total is None else total + part
        return total

    def start(m, carry):
        hidden = lax.dot_general(
            pf_ref[m], pair_ref[...], (((0,), (0,)), ((), ())), preferred_element_type=jnp.float32
        )
        hid_ref[m] = hidden
        spread(u_ref, m, hidden, 1)
        return carry

    lax.fori_loop(0, blocks, start, 0)

    def first(m, carry):
        inner = masked(m, jnp.maximum(conv(u_ref, m, near_ref, 0, 1), 0.0))
        spread(v_ref, m, inner, 1)
        return carry

    lax.fori_loop(0, blocks, first, 0)

    def second(m, carry):
        hidden = masked(m, hid_ref[m] + conv(v_ref, m, near_ref, 1, 1))
        hid_ref[m] = hidden
        spread(u_ref, m, hidden, 2)
        return carry

    lax.fori_loop(1, blocks - 1, second, 0)

    def third(m, carry):
        inner = masked(m, jnp.maximum(conv(u_ref, m, far_ref, 0, 2), 0.0))
        spread(v_ref, m, inner, 2)
        return carry

    lax.fori_loop(1, blocks - 1, third, 0)

    group = lax.broadcasted_iota(jnp.int32, (lanes, 128), 0) // size
    slot = lax.broadcasted_iota(jnp.int32, (lanes, 128), 1)

    def last(m, logits):
        hidden = hid_ref[m] + conv(v_ref, m, far_ref, 1, 2)
        weighed = hidden * head_ref[...]
        picks = jnp.where(slot == ROWS * (m - 2) + group, 1.0, 0.0).astype(bf16)
        for _ in range(3):
            coarse = weighed.astype(bf16)
            logits = logits + jnp.dot(coarse, picks, preferred_element_type=jnp.float32)
            weighed = weighed - coarse.astype(jnp.float32)
        return logits

    logits = lax.fori_loop(2, blocks - 2, last, jnp.zeros((residues, 128), jnp.float32))
    o_ref[...] = 1.0 / (1.0 + jnp.exp(-logits.T[: o_ref.shape[0]]))


def spread_taps(conv_weight):
    kinds, taps, size, _ = conv_weight.shape
    flipped = conv_weight.transpose(0, 1, 3, 2).reshape(kinds * taps, size, size)
    return pl.pallas_call(
        taps_kernel,
        out_shape=tuple(
            jax.ShapeDtypeStruct((2, 3, len(REACH[d]) * size, ROWS * size), conv_weight.dtype)
            for d in (1, 2)
        ),
        cost_estimate=cost(0, 6 << 20),
        name="spread_taps",
    )(flipped)


def contact_head(links, probs, pair_weight, taps, head_weight):
    _, chips, heads, rows, residues = probs.shape
    own_rows = residues // links.devices
    channels = pair_weight.shape[0]
    first_row = links.index * own_rows
    margin = 2 * ROWS
    band_rows = own_rows + 2 * margin
    blocks = band_rows // ROWS
    by_row = probs.transpose(1, 3, 0, 2, 4).reshape(residues, 2 * heads, residues)
    band_probs = lax.dynamic_slice_in_dim(
        jnp.pad(by_row, ((margin, margin), (0, 0), (0, 0))), first_row, band_rows, 0
    )
    band_cols = lax.dynamic_slice_in_dim(
        jnp.pad(probs, ((0, 0), (0, 0), (0, 0), (0, 0), (margin, margin))), first_row, band_rows, 4
    )
    band_cols = band_cols.transpose(4, 0, 2, 1, 3).reshape(band_rows, 2 * heads, residues)
    pair_features = (
        (band_probs.astype(jnp.float32) + band_cols.astype(jnp.float32)) * (residues * 0.5)
    ).astype(jnp.bfloat16)
    pair_features = pair_features.reshape(blocks, ROWS * 2 * heads, residues)
    pair = jnp.kron(jnp.eye(ROWS, dtype=pair_weight.dtype), pair_weight.T)
    head = jnp.tile(head_weight, ROWS)[None]
    lanes = ROWS * channels
    vmem = pl.BlockSpec(memory_space=pltpu.VMEM)
    work = 2 * residues * lanes * lanes * (13 * blocks + 17 * (blocks - 2))
    return pl.pallas_call(
        contact_kernel,
        out_shape=jax.ShapeDtypeStruct((own_rows, residues), jnp.float32),
        in_specs=[pl.BlockSpec(memory_space=pltpu.SMEM)] + [vmem] * 5,
        out_specs=vmem,
        scratch_shapes=[
            pltpu.VMEM((3, blocks, residues, lanes), jnp.bfloat16),
            pltpu.VMEM((3, blocks, residues, lanes), jnp.bfloat16),
            pltpu.VMEM((blocks, residues, lanes), jnp.float32),
        ],
        compiler_params=pltpu.CompilerParams(vmem_limit_bytes=48 << 20),
        cost_estimate=cost(work // 4, 4 << 20),
        name="contact_head",
    )(first_row.astype(jnp.int32).reshape(1), pair_features, pair, taps[0], taps[1], head)


def local(alignment, depth_count, qkv_weight, pair_weight, conv_weight, head_weight):
    seqs, residues, features = alignment.shape
    head_count = pair_weight.shape[1]
    size = features // head_count
    links = Links()
    depth = depth_count[0]
    half = links.core.astype(jnp.int32).reshape(1)
    use = jnp.clip(depth - links.index * seqs, 0, seqs).astype(jnp.int32).reshape(1)
    sent, own, values = projections(alignment, qkv_weight, half, use, head_count)
    other = links.send(sent, 0, 0, swap=True)
    order = jnp.stack(
        [links.at(dz, dy) for dz in range(links.tall) for dy in range(links.wide)]
    ).astype(jnp.int32)
    scale = size**-0.5 / jnp.sqrt(depth.astype(jnp.float32)) * LINK_SCALE
    scores = scores_of(own, other, order, scale.reshape(1), links.chips)
    summed = reduce_scatter(links, scores) * (1.0 / LINK_SCALE)
    probabilities = jax.nn.softmax(summed, axis=-1).astype(jnp.bfloat16)
    gathered = all_gather(links, probabilities)
    row_mix = row_mix_of(gathered, values, seqs, head_count)
    contacts = contact_head(links, gathered, pair_weight, spread_taps(conv_weight), head_weight)
    return (row_mix, contacts)


def solution(mesh):
    return jax.shard_map(
        local,
        mesh=mesh,
        in_specs=(P(("grp", "seq"), None, None), P("grp"), P(), P(), P(), P()),
        out_specs=(P(("grp", "seq"), None, None), P(("grp", "seq"), None)),
        check_vma=False,
    )
```

```python
import functools
import math

import jax
import jax.numpy as jnp
from jax import lax
from jax.experimental import pallas as pl
from jax.experimental.pallas import tpu as pltpu
from jax.sharding import PartitionSpec as P

EPSILON = 1e-05
LINK_SCALE = 2.0**-7


def grid_of(chips):
    width = 1
    while (2 * width) ** 2 <= chips:
        width *= 2
    return chips // width, width


def ring_of(chips):
    tall, wide = grid_of(chips)
    if tall % 2 or wide < 2:
        return list(range(chips))
    ring = [0]
    for row in range(tall):
        columns = range(1, wide) if row % 2 == 0 else range(wide - 1, 0, -1)
        ring += [row * wide + column for column in columns]
    return ring + [row * wide for row in range(tall - 1, 0, -1)]


def head_major(values, seqs, rows, size):
    out = []
    for head in range(values.shape[1] // size):
        pieces = [
            values[seq * rows : (seq + 1) * rows, head * size : (head + 1) * size]
            for seq in range(seqs)
        ]
        out.append(jnp.concatenate(pieces, axis=1))
    return out


def norm_send_kernel(half_ref, use_ref, x_ref, wq_ref, wk_ref, normed_ref, qk_ref):
    seqs, rows, width = x_ref.shape
    size = qk_ref.shape[3] // seqs
    values = x_ref[...].reshape(seqs * rows, width).astype(jnp.float32)
    average = jnp.mean(values, axis=-1, keepdims=True)
    centered = values - average
    variance = jnp.mean(centered * centered, axis=-1, keepdims=True)
    normed = (centered * lax.rsqrt(variance + EPSILON)).astype(jnp.bfloat16)
    normed_ref[...] = normed.reshape(seqs, rows, width)
    project(use_ref, normed, wq_ref, wk_ref, qk_ref, seqs, rows, size)


def own_kernel(half_ref, use_ref, normed_ref, wq_ref, wk_ref, qk_ref):
    seqs, rows, width = normed_ref.shape
    size = qk_ref.shape[3] // seqs
    normed = normed_ref[...].reshape(seqs * rows, width)
    project(use_ref, normed, wq_ref, wk_ref, qk_ref, seqs, rows, size)


def project(use_ref, normed, wq_ref, wk_ref, qk_ref, seqs, rows, size):
    q = jnp.dot(normed, wq_ref[...], preferred_element_type=jnp.float32).astype(jnp.bfloat16)
    for head, block in enumerate(head_major(q, seqs, rows, size)):
        lane = lax.broadcasted_iota(jnp.int32, block.shape, 1)
        qk_ref[0, head] = jnp.where(lane < use_ref[0] * size, block, jnp.zeros_like(block))
    k = jnp.dot(normed, wk_ref[...], preferred_element_type=jnp.float32).astype(jnp.bfloat16)
    for head, block in enumerate(head_major(k, seqs, rows, size)):
        qk_ref[1, head] = block


def value_kernel(normed_ref, w_ref, v_ref):
    seqs, rows, width = normed_ref.shape
    size = v_ref.shape[2] // seqs
    normed = normed_ref[...].reshape(seqs * rows, width)
    v = jnp.dot(normed, w_ref[...], preferred_element_type=jnp.float32).astype(jnp.bfloat16)
    for head, block in enumerate(head_major(v, seqs, rows, size)):
        v_ref[head] = block


def score_kernel(order_ref, scale_ref, own_ref, other_ref, s_ref):
    chips, _, rows, _ = s_ref.shape
    total = None
    for ref in (own_ref, other_ref):
        q = jnp.concatenate(
            [
                ref[0, 0, pl.ds(pl.multiple_of(order_ref[chip] * rows, rows), rows), :]
                for chip in range(chips)
            ],
            axis=0,
        )
        part = lax.dot_general(
            q, ref[1, 0], (((1,), (1,)), ((), ())), preferred_element_type=jnp.float32
        )
        total = part if total is None else total + part
    total = total * scale_ref[0]
    s_ref[...] = total.reshape(chips, 1, rows, total.shape[1])


def mix_kernel(p_ref, v_ref, o_ref):
    seqs = o_ref.shape[0]
    size = v_ref.shape[2] // seqs
    mixed = []
    for head in range(v_ref.shape[0]):
        probs = p_ref[0, :, head]
        probs = probs.reshape(probs.shape[0] * probs.shape[1], probs.shape[2])
        mixed.append(
            jnp.dot(probs, v_ref[head], preferred_element_type=jnp.float32).astype(jnp.bfloat16)
        )
    for seq in range(seqs):
        o_ref[seq] = jnp.concatenate(
            [block[:, seq * size : (seq + 1) * size] for block in mixed], axis=1
        )


def cost(flops, moved):
    return pl.CostEstimate(flops=int(flops), bytes_accessed=int(moved), transcendentals=0)


def projections(alignment, qkv_weight, half, use, head_count):
    seqs, residues, features = alignment.shape
    heads = head_count // 2
    size = features // head_count
    rows = 128 if residues % 128 == 0 else residues
    cols = heads * size
    steps = residues // rows
    bf16 = jnp.bfloat16
    x_spec = pl.BlockSpec((seqs, rows, features), lambda i, *_: (0, i, 0))
    qk_spec = pl.BlockSpec((2, heads, rows, seqs * size), lambda i, *_: (0, 0, i, 0))
    qk_shape = jax.ShapeDtypeStruct((2, heads, residues, seqs * size), bf16)
    params = pltpu.CompilerParams(vmem_limit_bytes=48 << 20)

    def weight_specs(pick):
        return [
            pl.BlockSpec((features, cols), lambda i, half, use: (0, pick(half[0]))),
            pl.BlockSpec((features, cols), lambda i, half, use: (0, 2 + pick(half[0]))),
        ]

    flops = 4 * seqs * residues * features * cols
    moved = 2 * (seqs * residues * features + 2 * features * cols + 2 * seqs * residues * cols)
    normed, sent = pl.pallas_call(
        norm_send_kernel,
        out_shape=(jax.ShapeDtypeStruct(alignment.shape, bf16), qk_shape),
        grid_spec=pltpu.PrefetchScalarGridSpec(
            num_scalar_prefetch=2,
            grid=(steps,),
            in_specs=[x_spec] + weight_specs(lambda half: 1 - half),
            out_specs=[x_spec, qk_spec],
        ),
        compiler_params=params,
        cost_estimate=cost(flops, moved + 2 * alignment.size),
        name="norm_send",
    )(half, use, alignment, qkv_weight, qkv_weight)
    own = pl.pallas_call(
        own_kernel,
        out_shape=qk_shape,
        grid_spec=pltpu.PrefetchScalarGridSpec(
            num_scalar_prefetch=2,
            grid=(steps,),
            in_specs=[x_spec] + weight_specs(lambda half: half),
            out_specs=qk_spec,
        ),
        compiler_params=params,
        cost_estimate=cost(flops, moved),
        name="own_project",
    )(half, use, normed, qkv_weight, qkv_weight)
    values = pl.pallas_call(
        value_kernel,
        out_shape=jax.ShapeDtypeStruct((head_count, residues, seqs * size), bf16),
        grid=(steps,),
        in_specs=[
            pl.BlockSpec((seqs, rows, features), lambda i: (0, i, 0)),
            pl.BlockSpec((features, features), lambda i: (0, 2)),
        ],
        out_specs=pl.BlockSpec((head_count, rows, seqs * size), lambda i: (0, i, 0)),
        compiler_params=params,
        cost_estimate=cost(flops, moved),
        name="value_project",
    )(normed, qkv_weight)
    return sent, own, values


def scores_of(own, other, order, scale, chips):
    _, heads, residues, inner = own.shape
    rows = residues // chips
    spec = pl.BlockSpec((2, 1, residues, inner), lambda h, *_: (0, h, 0, 0))
    return pl.pallas_call(
        score_kernel,
        out_shape=jax.ShapeDtypeStruct((chips, heads, rows, residues), jnp.float32),
        grid_spec=pltpu.PrefetchScalarGridSpec(
            num_scalar_prefetch=1,
            grid=(heads,),
            in_specs=[pl.BlockSpec(memory_space=pltpu.SMEM), spec, spec],
            out_specs=pl.BlockSpec((chips, 1, rows, residues), lambda h, *_: (0, h, 0, 0)),
        ),
        compiler_params=pltpu.CompilerParams(vmem_limit_bytes=32 << 20),
        cost_estimate=cost(4 * heads * residues * residues * inner, 4 * own.size + 4 * heads * residues**2),
        name="scores",
    )(order, scale, own, other)


def row_mix_of(probs, values, seqs, head_count):
    _, chips, heads, rows, residues = probs.shape
    inner = values.shape[2]
    size = inner // seqs
    pairs = heads // 2
    return pl.pallas_call(
        mix_kernel,
        out_shape=jax.ShapeDtypeStruct((seqs, residues, head_count * size), jnp.bfloat16),
        grid=(2 * pairs,),
        in_specs=[
            pl.BlockSpec((1, chips, 2, rows, residues), lambda g: (g // pairs, 0, g % pairs, 0, 0)),
            pl.BlockSpec((2, residues, inner), lambda g: (g, 0, 0)),
        ],
        out_specs=pl.BlockSpec((seqs, residues, 2 * size), lambda g: (0, 0, g)),
        compiler_params=pltpu.CompilerParams(vmem_limit_bytes=32 << 20),
        cost_estimate=cost(2 * probs.size * inner, 2 * (probs.size + 2 * values.size)),
        name="row_mix",
    )(probs, values)


class Links:
    def __init__(self):
        self.devices = lax.axis_size("seq")
        self.chips = self.devices // 2
        self.ring = ring_of(self.chips)
        self.index = lax.axis_index("seq")
        self.core = self.index % 2
        self.chip = self.index // 2
        places = [self.ring.index(chip) for chip in range(self.chips)]
        self.place = jnp.asarray(places, jnp.int32)[self.chip]

    def at(self, ahead):
        return jnp.asarray(self.ring, jnp.int32)[(self.place + ahead) % self.chips]

    def send(self, value, ahead):
        pairs = []
        for place, chip in enumerate(self.ring):
            target = self.ring[(place + ahead) % self.chips]
            pairs += [(2 * chip + core, 2 * target + core) for core in range(2)]
        return lax.ppermute(value, "seq", pairs)

    def swap(self, value):
        return lax.ppermute(value, "seq", [(i, i ^ 1) for i in range(self.devices)])


def reduce_scatter(links, scores, side):
    chips, _, rows, _ = scores.shape
    half = rows // 2
    low, high = slice(0, half), slice(half, rows)
    deep = chips // 2
    chains = [[(1, low), (-1, high)], [(1, high), (-1, low)]]

    def share(way, part, far):
        return scores[way * far % chips, :, part]

    moving = [None, None]
    gate = None
    side = list(side)
    done = []
    for far in range(deep, 0, -1):
        for group in range(2):
            if group == 1 and far == deep:
                continue
            chain = chains[group]
            if moving[group] is None:
                sums = [share(way, part, far).astype(jnp.float16) for way, part in chain]
            else:
                arrived = moving[group]
                if gate is not None:
                    arrived, _ = lax.optimization_barrier((arrived, gate))
                if side:
                    arrived, kept = lax.optimization_barrier((arrived, side.pop(0)))
                    done.append(kept)
                sums = [
                    (value.astype(jnp.float32) + share(way, part, far)).astype(jnp.float16)
                    for value, (way, part) in zip(arrived, chain)
                ]
            gate = sums
            moving[group] = [links.send(value, way) for value, (way, _) in zip(sums, chain)]
    (low_ahead, high_back), (high_ahead, low_back) = moving if deep > 1 else (moving[0], (0.0, 0.0))

    def settle(part, *arrived):
        total = scores[0, :, part]
        for value in arrived:
            total = total + value.astype(jnp.float32)
        return total

    if deep > 1:
        parts = [settle(low, low_ahead, low_back), settle(high, high_ahead, high_back)]
    else:
        parts = [settle(low, low_ahead), settle(high, high_back)]
    return jnp.concatenate(parts, axis=1), done + side


def all_gather(links, own, gathered):
    chips = links.chips
    half = own.shape[1] // 2
    deep = chips // 2
    pieces = [(0, 0, own)]
    ahead = back = own
    for far in range(1, deep):
        ahead = links.send(ahead, 1)
        back = links.send(back, -1)
        pieces += [(-far, 0, ahead), (far, 0, back)]
    pieces += [
        (-deep, 0, links.send(ahead[:, :half], 1)),
        (deep, half, links.send(back[:, half:], -1)),
    ]
    swapped = [links.swap(value) for _, _, value in pieces]
    for (far, row, value), other in zip(pieces, swapped):
        chip = links.at(far)
        where = (0, row, 0)
        gathered = lax.dynamic_update_slice(gathered, value[None, None], (links.core, chip) + where)
        gathered = lax.dynamic_update_slice(
            gathered, other[None, None], (1 - links.core, chip) + where
        )
    return gathered


ROWS = 4
REACH = {1: (0, 1, 2, 3, 4, -1), 2: (0, 1, 2, 3, -2, -1, 4, 5)}


def taps_kernel(w_ref, near_ref, far_ref):
    size = w_ref.shape[1]
    zero = jnp.zeros((size, size), w_ref.dtype)
    for dilation, out_ref in ((1, near_ref), (2, far_ref)):
        for which in range(2):
            base = 9 * (2 * (dilation - 1) + which)
            for col in range(3):
                for slot, row in enumerate(REACH[dilation]):
                    pieces = []
                    for out_row in range(ROWS):
                        step, rest = divmod(row - out_row, dilation)
                        live = rest == 0 and -1 <= step <= 1
                        pieces.append(w_ref[base + 3 * (step + 1) + col] if live else zero)
                    out_ref[which, col, slot * size : (slot + 1) * size, :] = jnp.concatenate(
                        pieces, axis=1
                    )


def contact_kernel(
    row_ref, pf_ref, pair_ref, near_ref, far_ref, head_ref, o_ref, u_ref, v_ref, hid_ref
):
    blocks, _, residues = pf_ref.shape
    lanes = pair_ref.shape[1]
    size = lanes // ROWS
    half = lanes // 2
    bf16 = jnp.bfloat16
    position = lax.broadcasted_iota(jnp.int32, (residues, lanes), 0)
    lane_row = lax.broadcasted_iota(jnp.int32, (1, lanes), 1) // size

    def masked(m, values):
        row = row_ref[0] + ROWS * (m - 2) + lane_row
        return jnp.where((row >= 0) & (row < residues), values, 0.0)

    def spread(ref, m, values, dilation):
        ref[1, m] = values.astype(bf16)
        left = jnp.where(position >= dilation, pltpu.roll(values, dilation, 0), 0.0)
        ref[0, m] = left.astype(bf16)
        right = jnp.where(
            position < residues - dilation, pltpu.roll(values, residues - dilation, 0), 0.0
        )
        ref[2, m] = right.astype(bf16)

    def conv(ref, m, w_ref, which, dilation):
        before = jnp.maximum(m - 1, 0)
        after = jnp.minimum(m + 1, blocks - 1)
        total = None
        for col in range(3):
            low = ref[col, before, :, half:]
            high = ref[col, after, :, :half]
            if dilation == 1:
                lane = lax.broadcasted_iota(jnp.int32, low.shape, 1)
                edge = [jnp.where(lane < size, high, low)]
            else:
                edge = [low, high]
            window = jnp.concatenate([ref[col, m]] + edge, axis=1)
            part = jnp.dot(window, w_ref[which, col], preferred_element_type=jnp.float32)
            total = part if total is None else total + part
        return total

    def start(m, carry):
        hidden = lax.dot_general(
            pf_ref[m], pair_ref[...], (((0,), (0,)), ((), ())), preferred_element_type=jnp.float32
        )
        hid_ref[m] = hidden
        spread(u_ref, m, hidden, 1)
        return carry

    lax.fori_loop(0, blocks, start, 0)

    def first(m, carry):
        inner = masked(m, jnp.maximum(conv(u_ref, m, near_ref, 0, 1), 0.0))
        spread(v_ref, m, inner, 1)
        return carry

    lax.fori_loop(0, blocks, first, 0)

    def second(m, carry):
        hidden = masked(m, hid_ref[m] + conv(v_ref, m, near_ref, 1, 1))
        hid_ref[m] = hidden
        spread(u_ref, m, hidden, 2)
        return carry

    lax.fori_loop(1, blocks - 1, second, 0)

    def third(m, carry):
        inner = masked(m, jnp.maximum(conv(u_ref, m, far_ref, 0, 2), 0.0))
        spread(v_ref, m, inner, 2)
        return carry

    lax.fori_loop(1, blocks - 1, third, 0)

    group = lax.broadcasted_iota(jnp.int32, (lanes, 128), 0) // size
    slot = lax.broadcasted_iota(jnp.int32, (lanes, 128), 1)

    def last(m, logits):
        hidden = hid_ref[m] + conv(v_ref, m, far_ref, 1, 2)
        weighed = hidden * head_ref[...]
        picks = jnp.where(slot == ROWS * (m - 2) + group, 1.0, 0.0).astype(bf16)
        for _ in range(3):
            coarse = weighed.astype(bf16)
            logits = logits + jnp.dot(coarse, picks, preferred_element_type=jnp.float32)
            weighed = weighed - coarse.astype(jnp.float32)
        return logits

    logits = lax.fori_loop(2, blocks - 2, last, jnp.zeros((residues, 128), jnp.float32))
    o_ref[...] = 1.0 / (1.0 + jnp.exp(-logits.T[: o_ref.shape[0]]))


def spread_taps(conv_weight):
    kinds, taps, size, _ = conv_weight.shape
    flipped = conv_weight.transpose(0, 1, 3, 2).reshape(kinds * taps, size, size)
    return pl.pallas_call(
        taps_kernel,
        out_shape=tuple(
            jax.ShapeDtypeStruct((2, 3, len(REACH[d]) * size, ROWS * size), conv_weight.dtype)
            for d in (1, 2)
        ),
        cost_estimate=cost(0, 6 << 20),
        name="spread_taps",
    )(flipped)


def contact_head(links, probs, pair_weight, taps, head_weight):
    _, chips, heads, rows, residues = probs.shape
    own_rows = residues // links.devices
    channels = pair_weight.shape[0]
    first_row = links.index * own_rows
    margin = 2 * ROWS
    band_rows = own_rows + 2 * margin
    blocks = band_rows // ROWS
    by_row = probs.transpose(1, 3, 0, 2, 4).reshape(residues, 2 * heads, residues)
    band_probs = lax.dynamic_slice_in_dim(
        jnp.pad(by_row, ((margin, margin), (0, 0), (0, 0))), first_row, band_rows, 0
    )
    band_cols = lax.dynamic_slice_in_dim(
        jnp.pad(probs, ((0, 0), (0, 0), (0, 0), (0, 0), (margin, margin))), first_row, band_rows, 4
    )
    band_cols = band_cols.transpose(4, 0, 2, 1, 3).reshape(band_rows, 2 * heads, residues)
    pair_features = (
        (band_probs.astype(jnp.float32) + band_cols.astype(jnp.float32)) * (residues * 0.5)
    ).astype(jnp.bfloat16)
    pair_features = pair_features.reshape(blocks, ROWS * 2 * heads, residues)
    pair = jnp.kron(jnp.eye(ROWS, dtype=pair_weight.dtype), pair_weight.T)
    head = jnp.tile(head_weight, ROWS)[None]
    lanes = ROWS * channels
    vmem = pl.BlockSpec(memory_space=pltpu.VMEM)
    work = 2 * residues * lanes * lanes * (13 * blocks + 17 * (blocks - 2))
    return pl.pallas_call(
        contact_kernel,
        out_shape=jax.ShapeDtypeStruct((own_rows, residues), jnp.float32),
        in_specs=[pl.BlockSpec(memory_space=pltpu.SMEM)] + [vmem] * 5,
        out_specs=vmem,
        scratch_shapes=[
            pltpu.VMEM((3, blocks, residues, lanes), jnp.bfloat16),
            pltpu.VMEM((3, blocks, residues, lanes), jnp.bfloat16),
            pltpu.VMEM((blocks, residues, lanes), jnp.float32),
        ],
        compiler_params=pltpu.CompilerParams(vmem_limit_bytes=48 << 20),
        cost_estimate=cost(work // 4, 4 << 20),
        name="contact_head",
    )(first_row.astype(jnp.int32).reshape(1), pair_features, pair, taps[0], taps[1], head)


def local(alignment, depth_count, qkv_weight, pair_weight, conv_weight, head_weight):
    seqs, residues, features = alignment.shape
    head_count = pair_weight.shape[1]
    size = features // head_count
    links = Links()
    depth = depth_count[0]
    half = links.core.astype(jnp.int32).reshape(1)
    use = jnp.clip(depth - links.index * seqs, 0, seqs).astype(jnp.int32).reshape(1)
    sent, own, values = projections(alignment, qkv_weight, half, use, head_count)
    other = links.swap(sent)
    order = jnp.stack([links.at(ahead) for ahead in range(links.chips)])
    scale = size**-0.5 / jnp.sqrt(depth.astype(jnp.float32)) * LINK_SCALE
    scores = scores_of(own, other, order, scale.reshape(1), links.chips)
    rows = residues // links.chips
    room = jnp.zeros((2, links.chips, head_count // 2, rows, residues), jnp.bfloat16)
    summed, (room, taps, values) = reduce_scatter(
        links, scores, (room, spread_taps(conv_weight), values)
    )
    probabilities = jax.nn.softmax(summed * (1.0 / LINK_SCALE), axis=-1).astype(jnp.bfloat16)
    gathered = all_gather(links, probabilities, room)
    row_mix = row_mix_of(gathered, values, seqs, head_count)
    contacts = contact_head(links, gathered, pair_weight, taps, head_weight)
    return (row_mix, contacts)


def solution(mesh):
    return jax.shard_map(
        local,
        mesh=mesh,
        in_specs=(P(("grp", "seq"), None, None), P("grp"), P(), P(), P(), P()),
        out_specs=(P(("grp", "seq"), None, None), P(("grp", "seq"), None)),
        check_vma=False,
    )
```

```python
import functools

import jax
import jax.numpy as jnp
from jax import lax
from jax.experimental import pallas as pl
from jax.experimental.pallas import tpu as pltpu
from jax.sharding import PartitionSpec as P

EPSILON = 1e-05
LINK_SCALE = 2.0**-7


def grid_of(chips):
    width = 1
    while (2 * width) ** 2 <= chips:
        width *= 2
    return chips // width, width


def ring_of(chips):
    tall, wide = grid_of(chips)
    if tall % 2 or wide < 2:
        return list(range(chips))
    ring = [0]
    for row in range(tall):
        columns = range(1, wide) if row % 2 == 0 else range(wide - 1, 0, -1)
        ring += [row * wide + column for column in columns]
    return ring + [row * wide for row in range(tall - 1, 0, -1)]


def head_major(values, seqs, rows, size):
    out = []
    for head in range(values.shape[1] // size):
        pieces = [
            values[seq * rows : (seq + 1) * rows, head * size : (head + 1) * size]
            for seq in range(seqs)
        ]
        out.append(jnp.concatenate(pieces, axis=1))
    return out


def ring_place(index_ref, table_ref, ahead):
    chips = table_ref.shape[0] // 2
    place = table_ref[lax.div(index_ref[0], 2)]
    return table_ref[chips + lax.rem(place + ahead, chips)]


def norm_send_kernel(index_ref, depth_ref, x_ref, wq_ref, wk_ref, normed_ref, qk_ref):
    seqs, rows, width = x_ref.shape
    size = qk_ref.shape[3] // seqs
    values = x_ref[...].reshape(seqs * rows, width).astype(jnp.float32)
    average = jnp.mean(values, axis=-1, keepdims=True)
    centered = values - average
    variance = jnp.mean(centered * centered, axis=-1, keepdims=True)
    normed = (centered * lax.rsqrt(variance + EPSILON)).astype(jnp.bfloat16)
    normed_ref[...] = normed.reshape(seqs, rows, width)
    project(index_ref, depth_ref, normed, wq_ref, wk_ref, qk_ref, seqs, rows, size)


def own_kernel(index_ref, depth_ref, normed_ref, wq_ref, wk_ref, qk_ref):
    seqs, rows, width = normed_ref.shape
    size = qk_ref.shape[3] // seqs
    normed = normed_ref[...].reshape(seqs * rows, width)
    project(index_ref, depth_ref, normed, wq_ref, wk_ref, qk_ref, seqs, rows, size)


def project(index_ref, depth_ref, normed, wq_ref, wk_ref, qk_ref, seqs, rows, size):
    q = jnp.dot(normed, wq_ref[...], preferred_element_type=jnp.float32).astype(jnp.bfloat16)
    for head, block in enumerate(head_major(q, seqs, rows, size)):
        lane = lax.broadcasted_iota(jnp.int32, block.shape, 1)
        in_use = (depth_ref[0] - index_ref[0] * seqs) * size
        qk_ref[0, head] = jnp.where(lane < in_use, block, jnp.zeros_like(block))
    k = jnp.dot(normed, wk_ref[...], preferred_element_type=jnp.float32).astype(jnp.bfloat16)
    for head, block in enumerate(head_major(k, seqs, rows, size)):
        qk_ref[1, head] = block


def value_kernel(normed_ref, w_ref, v_ref):
    seqs, rows, width = normed_ref.shape
    size = v_ref.shape[2] // seqs
    normed = normed_ref[...].reshape(seqs * rows, width)
    v = jnp.dot(normed, w_ref[...], preferred_element_type=jnp.float32).astype(jnp.bfloat16)
    for head, block in enumerate(head_major(v, seqs, rows, size)):
        v_ref[head] = block


def score_kernel(size, index_ref, table_ref, depth_ref, own_ref, other_ref, s_ref):
    chips, _, rows, residues = s_ref.shape
    depth = jnp.full((1, residues), depth_ref[0], jnp.int32).astype(jnp.float32)
    scale = size**-0.5 / jnp.sqrt(depth) * LINK_SCALE
    places = [
        pl.ds(pl.multiple_of(ring_place(index_ref, table_ref, ahead) * rows, rows), rows)
        for ahead in range(chips)
    ]
    total = None
    for ref in (own_ref, other_ref):
        q = jnp.concatenate([ref[0, 0, place, :] for place in places], axis=0)
        part = lax.dot_general(
            q, ref[1, 0], (((1,), (1,)), ((), ())), preferred_element_type=jnp.float32
        )
        total = part if total is None else total + part
    total = total * scale
    s_ref[...] = total.reshape(chips, 1, rows, total.shape[1])


def mix_kernel(index_ref, table_ref, p_ref, v_ref, o_ref):
    seqs = o_ref.shape[0]
    size = v_ref.shape[2] // seqs
    _, chips, _, rows, residues = p_ref.shape
    mixed = []
    for head in range(v_ref.shape[0]):
        probs = p_ref[0, :, head].reshape(chips * rows, residues)
        mixed.append(
            jnp.dot(probs, v_ref[head], preferred_element_type=jnp.float32).astype(jnp.bfloat16)
        )
    places = [
        pl.ds(pl.multiple_of(ring_place(index_ref, table_ref, ahead) * rows, rows), rows)
        for ahead in range(chips)
    ]
    for seq in range(seqs):
        joined = jnp.concatenate(
            [block[:, seq * size : (seq + 1) * size] for block in mixed], axis=1
        )
        for ahead, place in enumerate(places):
            o_ref[seq, place, :] = joined[ahead * rows : (ahead + 1) * rows]


def cost(flops, moved):
    return pl.CostEstimate(flops=int(flops), bytes_accessed=int(moved), transcendentals=0)


def projections(alignment, qkv_weight, index, depth_count, head_count):
    seqs, residues, features = alignment.shape
    heads = head_count // 2
    size = features // head_count
    rows = 128 if residues % 128 == 0 else residues
    cols = heads * size
    steps = residues // rows
    bf16 = jnp.bfloat16
    x_spec = pl.BlockSpec((seqs, rows, features), lambda i, *_: (0, i, 0))
    qk_spec = pl.BlockSpec((2, heads, rows, seqs * size), lambda i, *_: (0, 0, i, 0))
    qk_shape = jax.ShapeDtypeStruct((2, heads, residues, seqs * size), bf16)
    params = pltpu.CompilerParams(vmem_limit_bytes=48 << 20)

    def weight_specs(pick):
        return [
            pl.BlockSpec((features, cols), lambda i, index, _: (0, pick(lax.rem(index[0], 2)))),
            pl.BlockSpec((features, cols), lambda i, index, _: (0, 2 + pick(lax.rem(index[0], 2)))),
        ]

    flops = 4 * seqs * residues * features * cols
    moved = 2 * (seqs * residues * features + 2 * features * cols + 2 * seqs * residues * cols)
    normed, sent = pl.pallas_call(
        norm_send_kernel,
        out_shape=(jax.ShapeDtypeStruct(alignment.shape, bf16), qk_shape),
        grid_spec=pltpu.PrefetchScalarGridSpec(
            num_scalar_prefetch=2,
            grid=(steps,),
            in_specs=[x_spec] + weight_specs(lambda half: 1 - half),
            out_specs=[x_spec, qk_spec],
        ),
        compiler_params=params,
        cost_estimate=cost(flops, moved + 2 * alignment.size),
        name="norm_send",
    )(index, depth_count, alignment, qkv_weight, qkv_weight)
    own = pl.pallas_call(
        own_kernel,
        out_shape=qk_shape,
        grid_spec=pltpu.PrefetchScalarGridSpec(
            num_scalar_prefetch=2,
            grid=(steps,),
            in_specs=[x_spec] + weight_specs(lambda half: half),
            out_specs=qk_spec,
        ),
        compiler_params=params,
        cost_estimate=cost(flops, moved),
        name="own_project",
    )(index, depth_count, normed, qkv_weight, qkv_weight)
    values = pl.pallas_call(
        value_kernel,
        out_shape=jax.ShapeDtypeStruct((head_count, residues, seqs * size), bf16),
        grid=(steps,),
        in_specs=[
            pl.BlockSpec((seqs, rows, features), lambda i: (0, i, 0)),
            pl.BlockSpec((features, features), lambda i: (0, 2)),
        ],
        out_specs=pl.BlockSpec((head_count, rows, seqs * size), lambda i: (0, i, 0)),
        compiler_params=params,
        cost_estimate=cost(flops, moved),
        name="value_project",
    )(normed, qkv_weight)
    return sent, own, values


def scores_of(own, other, index, table, depth_count, size):
    _, heads, residues, inner = own.shape
    chips = table.shape[0] // 2
    rows = residues // chips
    spec = pl.BlockSpec((2, 1, residues, inner), lambda h, *_: (0, h, 0, 0))
    return pl.pallas_call(
        functools.partial(score_kernel, size),
        out_shape=jax.ShapeDtypeStruct((chips, heads, rows, residues), jnp.float32),
        grid_spec=pltpu.PrefetchScalarGridSpec(
            num_scalar_prefetch=3,
            grid=(heads,),
            in_specs=[spec, spec],
            out_specs=pl.BlockSpec((chips, 1, rows, residues), lambda h, *_: (0, h, 0, 0)),
        ),
        compiler_params=pltpu.CompilerParams(vmem_limit_bytes=32 << 20),
        cost_estimate=cost(4 * heads * residues * residues * inner, 4 * own.size + 4 * heads * residues**2),
        name="scores",
    )(index, table, depth_count, own, other)


def row_mix_of(probs, values, index, table, seqs, head_count):
    _, chips, heads, rows, residues = probs.shape
    inner = values.shape[2]
    size = inner // seqs
    pairs = heads // 2

    def pair_at(g, index):
        core = lax.rem(index[0] + lax.div(g, pairs), 2)
        return core * pairs + lax.rem(g, pairs)

    return pl.pallas_call(
        mix_kernel,
        out_shape=jax.ShapeDtypeStruct((seqs, residues, head_count * size), jnp.bfloat16),
        grid_spec=pltpu.PrefetchScalarGridSpec(
            num_scalar_prefetch=2,
            grid=(2 * pairs,),
            in_specs=[
                pl.BlockSpec(
                    (1, chips, 2, rows, residues),
                    lambda g, *_: (lax.div(g, pairs), 0, lax.rem(g, pairs), 0, 0),
                ),
                pl.BlockSpec((2, residues, inner), lambda g, index, _: (pair_at(g, index), 0, 0)),
            ],
            out_specs=pl.BlockSpec(
                (seqs, residues, 2 * size), lambda g, index, _: (0, 0, pair_at(g, index))
            ),
        ),
        compiler_params=pltpu.CompilerParams(vmem_limit_bytes=32 << 20),
        cost_estimate=cost(2 * probs.size * inner, 2 * (probs.size + 2 * values.size)),
        name="row_mix",
    )(index, table, probs, values)


class Links:
    def __init__(self):
        self.devices = lax.axis_size("seq")
        self.chips = self.devices // 2
        self.ring = ring_of(self.chips)
        places = [self.ring.index(chip) for chip in range(self.chips)]
        self.table = jnp.asarray(places + self.ring, jnp.int32)
        self.index = lax.axis_index("seq").astype(jnp.int32).reshape(1)

    def send(self, value, ahead):
        pairs = []
        for place, chip in enumerate(self.ring):
            target = self.ring[(place + ahead) % self.chips]
            pairs += [(2 * chip + core, 2 * target + core) for core in range(2)]
        return lax.ppermute(value, "seq", pairs)

    def swap(self, value):
        return lax.ppermute(value, "seq", [(i, i ^ 1) for i in range(self.devices)])


def reduce_scatter(links, scores, side):
    chips, _, rows, _ = scores.shape
    half = rows // 2
    low, high = slice(0, half), slice(half, rows)
    deep = chips // 2
    chains = [[(1, low), (-1, high)], [(1, high), (-1, low)]]

    def share(way, part, far):
        return scores[way * far % chips, :, part]

    moving = [None, None]
    gate = None
    side = list(side)
    done = []
    for far in range(deep, 0, -1):
        for group in range(2):
            if group == 1 and far == deep:
                continue
            chain = chains[group]
            if moving[group] is None:
                sums = [share(way, part, far).astype(jnp.float16) for way, part in chain]
            else:
                arrived = moving[group]
                if gate is not None:
                    arrived, _ = lax.optimization_barrier((arrived, gate))
                if side:
                    arrived, kept = lax.optimization_barrier((arrived, side.pop(0)))
                    done.append(kept)
                sums = [
                    (value.astype(jnp.float32) + share(way, part, far)).astype(jnp.float16)
                    for value, (way, part) in zip(arrived, chain)
                ]
            gate = sums
            moving[group] = [links.send(value, way) for value, (way, _) in zip(sums, chain)]
    (low_ahead, high_back), (high_ahead, low_back) = moving if deep > 1 else (moving[0], (0.0, 0.0))

    def settle(part, *arrived):
        total = scores[0, :, part]
        for value in arrived:
            total = total + value.astype(jnp.float32)
        return total

    if deep > 1:
        parts = [settle(low, low_ahead, low_back), settle(high, high_ahead, high_back)]
    else:
        parts = [settle(low, low_ahead), settle(high, high_back)]
    return jnp.concatenate(parts, axis=1), done + side


def all_gather(links, own, gathered):
    chips = links.chips
    half = own.shape[1] // 2
    deep = chips // 2
    pieces = [(0, 0, own)]
    ahead = back = own
    for far in range(1, deep):
        ahead = links.send(ahead, 1)
        back = links.send(back, -1)
        pieces += [(chips - far, 0, ahead), (far, 0, back)]
    pieces += [
        (deep, 0, links.send(ahead[:, :half], 1)),
        (deep, half, links.send(back[:, half:], -1)),
    ]
    swapped = [links.swap(value) for _, _, value in pieces]
    for (far, row, value), other in zip(pieces, swapped):
        for core, piece in enumerate((value, other)):
            gathered = lax.dynamic_update_slice(gathered, piece[None, None], (core, far, 0, row, 0))
    return gathered


ROWS = 4
REACH = {1: (0, 1, 2, 3, 4, -1), 2: (0, 1, 2, 3, -2, -1, 4, 5)}


def taps_kernel(w_ref, near_ref, far_ref):
    size = w_ref.shape[1]
    zero = jnp.zeros((size, size), w_ref.dtype)
    for dilation, out_ref in ((1, near_ref), (2, far_ref)):
        for which in range(2):
            base = 9 * (2 * (dilation - 1) + which)
            for col in range(3):
                for slot, row in enumerate(REACH[dilation]):
                    pieces = []
                    for out_row in range(ROWS):
                        step, rest = divmod(row - out_row, dilation)
                        live = rest == 0 and -1 <= step <= 1
                        pieces.append(w_ref[base + 3 * (step + 1) + col] if live else zero)
                    out_ref[which, col, slot * size : (slot + 1) * size, :] = jnp.concatenate(
                        pieces, axis=1
                    )


def contact_kernel(
    index_ref, pf_ref, pair_ref, near_ref, far_ref, head_ref, o_ref, u_ref, v_ref, hid_ref
):
    blocks, _, residues = pf_ref.shape
    lanes = pair_ref.shape[1]
    size = lanes // ROWS
    half = lanes // 2
    bf16 = jnp.bfloat16
    position = lax.broadcasted_iota(jnp.int32, (residues, lanes), 0)
    lane_row = lax.broadcasted_iota(jnp.int32, (1, lanes), 1) // size

    def masked(m, values):
        row = index_ref[0] * o_ref.shape[0] + ROWS * (m - 2) + lane_row
        return jnp.where((row >= 0) & (row < residues), values, 0.0)

    def spread(ref, m, values, dilation):
        ref[1, m] = values.astype(bf16)
        left = jnp.where(position >= dilation, pltpu.roll(values, dilation, 0), 0.0)
        ref[0, m] = left.astype(bf16)
        right = jnp.where(
            position < residues - dilation, pltpu.roll(values, residues - dilation, 0), 0.0
        )
        ref[2, m] = right.astype(bf16)

    def conv(ref, m, w_ref, which, dilation):
        before = jnp.maximum(m - 1, 0)
        after = jnp.minimum(m + 1, blocks - 1)
        total = None
        for col in range(3):
            low = ref[col, before, :, half:]
            high = ref[col, after, :, :half]
            if dilation == 1:
                lane = lax.broadcasted_iota(jnp.int32, low.shape, 1)
                edge = [jnp.where(lane < size, high, low)]
            else:
                edge = [low, high]
            window = jnp.concatenate([ref[col, m]] + edge, axis=1)
            part = jnp.dot(window, w_ref[which, col], preferred_element_type=jnp.float32)
            total = part if total is None else total + part
        return total

    def start(m, carry):
        hidden = lax.dot_general(
            pf_ref[m], pair_ref[...], (((0,), (0,)), ((), ())), preferred_element_type=jnp.float32
        )
        hid_ref[m] = hidden
        spread(u_ref, m, hidden, 1)
        return carry

    lax.fori_loop(0, blocks, start, 0)

    def first(m, carry):
        inner = masked(m, jnp.maximum(conv(u_ref, m, near_ref, 0, 1), 0.0))
        spread(v_ref, m, inner, 1)
        return carry

    lax.fori_loop(0, blocks, first, 0)

    def second(m, carry):
        hidden = masked(m, hid_ref[m] + conv(v_ref, m, near_ref, 1, 1))
        hid_ref[m] = hidden
        spread(u_ref, m, hidden, 2)
        return carry

    lax.fori_loop(1, blocks - 1, second, 0)

    def third(m, carry):
        inner = masked(m, jnp.maximum(conv(u_ref, m, far_ref, 0, 2), 0.0))
        spread(v_ref, m, inner, 2)
        return carry

    lax.fori_loop(1, blocks - 1, third, 0)

    group = lax.broadcasted_iota(jnp.int32, (lanes, 128), 0) // size
    slot = lax.broadcasted_iota(jnp.int32, (lanes, 128), 1)

    def last(m, logits):
        hidden = hid_ref[m] + conv(v_ref, m, far_ref, 1, 2)
        weighed = hidden * head_ref[...]
        picks = jnp.where(slot == ROWS * (m - 2) + group, 1.0, 0.0).astype(bf16)
        for _ in range(3):
            coarse = weighed.astype(bf16)
            logits = logits + jnp.dot(coarse, picks, preferred_element_type=jnp.float32)
            weighed = weighed - coarse.astype(jnp.float32)
        return logits

    logits = lax.fori_loop(2, blocks - 2, last, jnp.zeros((residues, 128), jnp.float32))
    o_ref[...] = 1.0 / (1.0 + jnp.exp(-logits.T[: o_ref.shape[0]]))


def spread_taps(conv_weight):
    kinds, taps, size, _ = conv_weight.shape
    flipped = conv_weight.transpose(0, 1, 3, 2).reshape(kinds * taps, size, size)
    return pl.pallas_call(
        taps_kernel,
        out_shape=tuple(
            jax.ShapeDtypeStruct((2, 3, len(REACH[d]) * size, ROWS * size), conv_weight.dtype)
            for d in (1, 2)
        ),
        cost_estimate=cost(0, 6 << 20),
        name="spread_taps",
    )(flipped)


def window_kernel(index_ref, table_ref, p_ref, pf_ref, cols_ref, rows_ref):
    cores, chips, heads, rows, residues = p_ref.shape
    blocks, taken, _ = pf_ref.shape
    band = ROWS * blocks
    own_rows = band - 4 * ROWS
    first = index_ref[0] * own_rows - 2 * ROWS
    wide = cols_ref.shape[1] // (cores * heads)
    tall = rows_ref.shape[0] // (cores * heads)
    left = jnp.clip(lax.div(first, 128) * 128, 0, residues - wide)
    top = jnp.clip(lax.div(first, rows) * rows, 0, residues - tall)
    core = lax.rem(index_ref[0], 2)
    place = table_ref[lax.div(index_ref[0], 2)]
    lanes = pl.ds(pl.multiple_of(left, 128), wide)
    for ahead in range(chips):
        chip = ring_place(index_ref, table_ref, ahead)
        there = pl.ds(pl.multiple_of(chip * rows, rows), rows)
        for side in range(cores):
            for head in range(heads):
                slot = side * heads + head
                cols_ref[there, slot * wide : (slot + 1) * wide] = p_ref[side, ahead, head, :, lanes]
    for step in range(tall // rows):
        ahead = lax.rem(table_ref[lax.div(top, rows) + step] - place + chips, chips)
        for side in range(cores):
            for head in range(heads):
                start = (side * heads + head) * tall + step * rows
                rows_ref[start : start + rows, :] = p_ref[side, ahead, head]

    def picks(extent, base, out_rows, start):
        count = cores * heads * extent
        at = lax.broadcasted_iota(jnp.int32, (1, count), 1)
        slot = lax.div(at, extent)
        side = lax.div(slot, heads)
        head = lax.rem(side + core, 2) * heads + slot - side * heads
        have = head * 2048 + base + at - slot * extent
        out = start + lax.broadcasted_iota(jnp.int32, (out_rows, 1), 0)
        block = lax.div(out, taken)
        rest = out - block * taken
        head = lax.div(rest, ROWS)
        row = first + ROWS * block + rest - head * ROWS
        want = jnp.where((row >= 0) & (row < residues), head * 2048 + row, -1)
        return jnp.where(want == have, 1.0, 0.0).astype(jnp.bfloat16)

    step = 3 if blocks % 3 == 0 else 1
    for block in range(0, blocks, step):
        by_col = lax.dot_general(
            picks(wide, left, step * taken, block * taken),
            cols_ref[...],
            (((1,), (1,)), ((), ())),
            preferred_element_type=jnp.float32,
        )
        by_row = jnp.dot(
            picks(tall, top, step * taken, block * taken),
            rows_ref[...],
            preferred_element_type=jnp.float32,
        )
        both = ((by_col + by_row) * (residues * 0.5)).astype(jnp.bfloat16)
        pf_ref[block : block + step] = both.reshape(step, taken, residues)


def contact_head(links, probs, pair_weight, taps, head_weight):
    cores, chips, heads, rows, residues = probs.shape
    own_rows = residues // links.devices
    blocks = own_rows // ROWS + 4
    count = cores * heads
    wide = min(256, residues)
    tall = max(2 * rows, 64)
    smem = pl.BlockSpec(memory_space=pltpu.SMEM)
    vmem = pl.BlockSpec(memory_space=pltpu.VMEM)
    pair_features = pl.pallas_call(
        window_kernel,
        out_shape=jax.ShapeDtypeStruct((blocks, ROWS * count, residues), jnp.bfloat16),
        in_specs=[smem, smem, vmem],
        out_specs=vmem,
        scratch_shapes=[
            pltpu.VMEM((residues, count * wide), jnp.bfloat16),
            pltpu.VMEM((count * tall, residues), jnp.bfloat16),
        ],
        compiler_params=pltpu.CompilerParams(vmem_limit_bytes=40 << 20),
        cost_estimate=cost(2 * blocks * ROWS * count**2 * residues * (wide + tall), 2 * probs.size),
        name="pair_window",
    )(links.index, links.table, probs)
    return contact_call(links.index, pair_features, pair_weight, taps, head_weight, own_rows)


def contact_call(index, pair_features, pair_weight, taps, head_weight, own_rows):
    blocks, _, residues = pair_features.shape
    channels = pair_weight.shape[0]
    same = jnp.eye(ROWS, dtype=pair_weight.dtype)
    pair = (pair_weight.T[:, None, None, :] * same[None, :, :, None]).reshape(-1, ROWS * channels)
    head = jnp.tile(head_weight, ROWS)[None]
    lanes = ROWS * channels
    vmem = pl.BlockSpec(memory_space=pltpu.VMEM)
    work = 2 * residues * lanes * lanes * (13 * blocks + 17 * (blocks - 2))
    return pl.pallas_call(
        contact_kernel,
        out_shape=jax.ShapeDtypeStruct((own_rows, residues), jnp.float32),
        in_specs=[pl.BlockSpec(memory_space=pltpu.SMEM)] + [vmem] * 5,
        out_specs=vmem,
        scratch_shapes=[
            pltpu.VMEM((3, blocks, residues, lanes), jnp.bfloat16),
            pltpu.VMEM((3, blocks, residues, lanes), jnp.bfloat16),
            pltpu.VMEM((blocks, residues, lanes), jnp.float32),
        ],
        compiler_params=pltpu.CompilerParams(vmem_limit_bytes=48 << 20),
        cost_estimate=cost(work // 4, 4 << 20),
        name="contact_head",
    )(index, pair_features, pair, taps[0], taps[1], head)


def local(alignment, depth_count, qkv_weight, pair_weight, conv_weight, head_weight):
    seqs, residues, features = alignment.shape
    head_count = pair_weight.shape[1]
    size = features // head_count
    links = Links()
    sent, own, values = projections(alignment, qkv_weight, links.index, depth_count, head_count)
    other = links.swap(sent)
    scores = scores_of(own, other, links.index, links.table, depth_count, size)
    rows = residues // links.chips
    room = jnp.zeros((2, links.chips, head_count // 2, rows, residues), jnp.bfloat16)
    summed, (room, taps, values) = reduce_scatter(
        links, scores, (room, spread_taps(conv_weight), values)
    )
    probabilities = jax.nn.softmax(summed * (1.0 / LINK_SCALE), axis=-1).astype(jnp.bfloat16)
    gathered = all_gather(links, probabilities, room)
    row_mix = row_mix_of(gathered, values, links.index, links.table, seqs, head_count)
    contacts = contact_head(links, gathered, pair_weight, taps, head_weight)
    return (row_mix, contacts)


def solution(mesh):
    return jax.shard_map(
        local,
        mesh=mesh,
        in_specs=(P(("grp", "seq"), None, None), P("grp"), P(), P(), P(), P()),
        out_specs=(P(("grp", "seq"), None, None), P(("grp", "seq"), None)),
        check_vma=False,
    )
```

```python
import functools

import jax
import jax.numpy as jnp
from jax import lax
from jax.experimental import pallas as pl
from jax.experimental.pallas import tpu as pltpu
from jax.sharding import PartitionSpec as P

EPSILON = 1e-05
LINK_SCALE = 2.0**-7


def grid_of(chips):
    width = 1
    while (2 * width) ** 2 <= chips:
        width *= 2
    return chips // width, width


def ring_of(chips):
    tall, wide = grid_of(chips)
    if tall % 2 or wide < 2:
        return list(range(chips))
    ring = [0]
    for row in range(tall):
        columns = range(1, wide) if row % 2 == 0 else range(wide - 1, 0, -1)
        ring += [row * wide + column for column in columns]
    return ring + [row * wide for row in range(tall - 1, 0, -1)]


def head_major(values, seqs, rows, size):
    out = []
    for head in range(values.shape[1] // size):
        pieces = [
            values[seq * rows : (seq + 1) * rows, head * size : (head + 1) * size]
            for seq in range(seqs)
        ]
        out.append(jnp.concatenate(pieces, axis=1))
    return out


def ring_place(index_ref, table_ref, ahead):
    chips = table_ref.shape[0] // 2
    place = table_ref[lax.div(index_ref[0], 2)]
    return table_ref[chips + lax.rem(place + ahead, chips)]


def norm_send_kernel(index_ref, depth_ref, x_ref, wq_ref, wk_ref, normed_ref, qk_ref):
    seqs, rows, width = x_ref.shape
    size = qk_ref.shape[3] // seqs
    values = x_ref[...].reshape(seqs * rows, width).astype(jnp.float32)
    average = jnp.mean(values, axis=-1, keepdims=True)
    centered = values - average
    variance = jnp.mean(centered * centered, axis=-1, keepdims=True)
    normed = (centered * lax.rsqrt(variance + EPSILON)).astype(jnp.bfloat16)
    normed_ref[...] = normed.reshape(seqs, rows, width)
    project(index_ref, depth_ref, normed, wq_ref, wk_ref, qk_ref, seqs, rows, size)


def own_kernel(index_ref, depth_ref, normed_ref, wq_ref, wk_ref, qk_ref):
    seqs, rows, width = normed_ref.shape
    size = qk_ref.shape[3] // seqs
    normed = normed_ref[...].reshape(seqs * rows, width)
    project(index_ref, depth_ref, normed, wq_ref, wk_ref, qk_ref, seqs, rows, size)


def project(index_ref, depth_ref, normed, wq_ref, wk_ref, qk_ref, seqs, rows, size):
    q = jnp.dot(normed, wq_ref[...], preferred_element_type=jnp.float32).astype(jnp.bfloat16)
    for head, block in enumerate(head_major(q, seqs, rows, size)):
        lane = lax.broadcasted_iota(jnp.int32, block.shape, 1)
        in_use = (depth_ref[0] - index_ref[0] * seqs) * size
        qk_ref[0, head] = jnp.where(lane < in_use, block, jnp.zeros_like(block))
    k = jnp.dot(normed, wk_ref[...], preferred_element_type=jnp.float32).astype(jnp.bfloat16)
    for head, block in enumerate(head_major(k, seqs, rows, size)):
        qk_ref[1, head] = block


def value_kernel(normed_ref, w_ref, v_ref):
    seqs, rows, width = normed_ref.shape
    size = v_ref.shape[2] // seqs
    normed = normed_ref[...].reshape(seqs * rows, width)
    v = jnp.dot(normed, w_ref[...], preferred_element_type=jnp.float32).astype(jnp.bfloat16)
    for head, block in enumerate(head_major(v, seqs, rows, size)):
        v_ref[head] = block


def score_kernel(size, index_ref, table_ref, depth_ref, own_ref, other_ref, s_ref):
    chips, _, rows, residues = s_ref.shape
    depth = jnp.full((1, residues), depth_ref[0], jnp.int32).astype(jnp.float32)
    scale = size**-0.5 / jnp.sqrt(depth) * LINK_SCALE
    places = [
        pl.ds(pl.multiple_of(ring_place(index_ref, table_ref, ahead) * rows, rows), rows)
        for ahead in range(chips)
    ]
    total = None
    for ref in (own_ref, other_ref):
        q = jnp.concatenate([ref[0, 0, place, :] for place in places], axis=0)
        part = lax.dot_general(
            q, ref[1, 0], (((1,), (1,)), ((), ())), preferred_element_type=jnp.float32
        )
        total = part if total is None else total + part
    total = total * scale
    s_ref[...] = total.reshape(chips, 1, rows, total.shape[1])


def mix_kernel(index_ref, table_ref, p_ref, v_ref, o_ref):
    seqs = o_ref.shape[0]
    size = v_ref.shape[2] // seqs
    _, chips, _, rows, residues = p_ref.shape
    mixed = []
    for head in range(v_ref.shape[0]):
        probs = p_ref[0, :, head].reshape(chips * rows, residues)
        mixed.append(
            jnp.dot(probs, v_ref[head], preferred_element_type=jnp.float32).astype(jnp.bfloat16)
        )
    places = [
        pl.ds(pl.multiple_of(ring_place(index_ref, table_ref, ahead) * rows, rows), rows)
        for ahead in range(chips)
    ]
    for seq in range(seqs):
        joined = jnp.concatenate(
            [block[:, seq * size : (seq + 1) * size] for block in mixed], axis=1
        )
        for ahead, place in enumerate(places):
            o_ref[seq, place, :] = joined[ahead * rows : (ahead + 1) * rows]


def cost(flops, moved):
    return pl.CostEstimate(flops=int(flops), bytes_accessed=int(moved), transcendentals=0)


def projections(alignment, qkv_weight, index, depth_count, head_count):
    seqs, residues, features = alignment.shape
    heads = head_count // 2
    size = features // head_count
    rows = 128 if residues % 128 == 0 else residues
    cols = heads * size
    steps = residues // rows
    bf16 = jnp.bfloat16
    x_spec = pl.BlockSpec((seqs, rows, features), lambda i, *_: (0, i, 0))
    qk_spec = pl.BlockSpec((2, heads, rows, seqs * size), lambda i, *_: (0, 0, i, 0))
    qk_shape = jax.ShapeDtypeStruct((2, heads, residues, seqs * size), bf16)
    params = pltpu.CompilerParams(vmem_limit_bytes=48 << 20)

    def weight_specs(pick):
        return [
            pl.BlockSpec((features, cols), lambda i, index, _: (0, pick(lax.rem(index[0], 2)))),
            pl.BlockSpec((features, cols), lambda i, index, _: (0, 2 + pick(lax.rem(index[0], 2)))),
        ]

    flops = 4 * seqs * residues * features * cols
    moved = 2 * (seqs * residues * features + 2 * features * cols + 2 * seqs * residues * cols)
    normed, sent = pl.pallas_call(
        norm_send_kernel,
        out_shape=(jax.ShapeDtypeStruct(alignment.shape, bf16), qk_shape),
        grid_spec=pltpu.PrefetchScalarGridSpec(
            num_scalar_prefetch=2,
            grid=(steps,),
            in_specs=[x_spec] + weight_specs(lambda half: 1 - half),
            out_specs=[x_spec, qk_spec],
        ),
        compiler_params=params,
        cost_estimate=cost(flops, moved + 2 * alignment.size),
        name="norm_send",
    )(index, depth_count, alignment, qkv_weight, qkv_weight)
    own = pl.pallas_call(
        own_kernel,
        out_shape=qk_shape,
        grid_spec=pltpu.PrefetchScalarGridSpec(
            num_scalar_prefetch=2,
            grid=(steps,),
            in_specs=[x_spec] + weight_specs(lambda half: half),
            out_specs=qk_spec,
        ),
        compiler_params=params,
        cost_estimate=cost(flops, moved),
        name="own_project",
    )(index, depth_count, normed, qkv_weight, qkv_weight)
    return sent, own, normed


def value_projection(normed, qkv_weight, head_count):
    seqs, residues, features = normed.shape
    size = features // head_count
    rows = 128 if residues % 128 == 0 else residues
    steps = residues // rows
    flops = 2 * seqs * residues * features * features
    moved = 2 * (2 * seqs * residues * features + features * features)
    bf16 = jnp.bfloat16
    params = pltpu.CompilerParams(vmem_limit_bytes=48 << 20)
    return pl.pallas_call(
        value_kernel,
        out_shape=jax.ShapeDtypeStruct((head_count, residues, seqs * size), bf16),
        grid=(steps,),
        in_specs=[
            pl.BlockSpec((seqs, rows, features), lambda i: (0, i, 0)),
            pl.BlockSpec((features, features), lambda i: (0, 2)),
        ],
        out_specs=pl.BlockSpec((head_count, rows, seqs * size), lambda i: (0, i, 0)),
        compiler_params=params,
        cost_estimate=cost(flops, moved),
        name="value_project",
    )(normed, qkv_weight)


def scores_of(own, other, index, table, depth_count, size):
    _, heads, residues, inner = own.shape
    chips = table.shape[0] // 2
    rows = residues // chips
    spec = pl.BlockSpec((2, 1, residues, inner), lambda h, *_: (0, h, 0, 0))
    return pl.pallas_call(
        functools.partial(score_kernel, size),
        out_shape=jax.ShapeDtypeStruct((chips, heads, rows, residues), jnp.float32),
        grid_spec=pltpu.PrefetchScalarGridSpec(
            num_scalar_prefetch=3,
            grid=(heads,),
            in_specs=[spec, spec],
            out_specs=pl.BlockSpec((chips, 1, rows, residues), lambda h, *_: (0, h, 0, 0)),
        ),
        compiler_params=pltpu.CompilerParams(vmem_limit_bytes=32 << 20),
        cost_estimate=cost(4 * heads * residues * residues * inner, 4 * own.size + 4 * heads * residues**2),
        name="scores",
    )(index, table, depth_count, own, other)


def row_mix_of(probs, values, index, table, seqs, head_count):
    _, chips, heads, rows, residues = probs.shape
    inner = values.shape[2]
    size = inner // seqs
    pairs = heads // 2

    def pair_at(g, index):
        core = lax.rem(index[0] + lax.div(g, pairs), 2)
        return core * pairs + lax.rem(g, pairs)

    return pl.pallas_call(
        mix_kernel,
        out_shape=jax.ShapeDtypeStruct((seqs, residues, head_count * size), jnp.bfloat16),
        grid_spec=pltpu.PrefetchScalarGridSpec(
            num_scalar_prefetch=2,
            grid=(2 * pairs,),
            in_specs=[
                pl.BlockSpec(
                    (1, chips, 2, rows, residues),
                    lambda g, *_: (lax.div(g, pairs), 0, lax.rem(g, pairs), 0, 0),
                ),
                pl.BlockSpec((2, residues, inner), lambda g, index, _: (pair_at(g, index), 0, 0)),
            ],
            out_specs=pl.BlockSpec(
                (seqs, residues, 2 * size), lambda g, index, _: (0, 0, pair_at(g, index))
            ),
        ),
        compiler_params=pltpu.CompilerParams(vmem_limit_bytes=32 << 20),
        cost_estimate=cost(2 * probs.size * inner, 2 * (probs.size + 2 * values.size)),
        name="row_mix",
    )(index, table, probs, values)


class Links:
    def __init__(self):
        self.devices = lax.axis_size("seq")
        self.chips = self.devices // 2
        self.ring = ring_of(self.chips)
        places = [self.ring.index(chip) for chip in range(self.chips)]
        self.table = jnp.asarray(places + self.ring, jnp.int32)
        self.index = lax.axis_index("seq").astype(jnp.int32).reshape(1)

    def send(self, value, ahead):
        pairs = []
        for place, chip in enumerate(self.ring):
            target = self.ring[(place + ahead) % self.chips]
            pairs += [(2 * chip + core, 2 * target + core) for core in range(2)]
        return lax.ppermute(value, "seq", pairs)

    def swap(self, value):
        return lax.ppermute(value, "seq", [(i, i ^ 1) for i in range(self.devices)])


def reduce_scatter(links, scores):
    chips, _, rows, _ = scores.shape
    half = rows // 2
    low, high = slice(0, half), slice(half, rows)
    deep = chips // 2
    chains = [[(1, low), (-1, high)], [(1, high), (-1, low)]]

    def share(way, part, far):
        return scores[way * far % chips, :, part]

    moving = [None, None]
    gate = None
    for far in range(deep, 0, -1):
        for group in range(2):
            if group == 1 and far == deep:
                continue
            chain = chains[group]
            if moving[group] is None:
                sums = [share(way, part, far).astype(jnp.float16) for way, part in chain]
            else:
                arrived, _ = lax.optimization_barrier((moving[group], gate))
                sums = [
                    (value.astype(jnp.float32) + share(way, part, far)).astype(jnp.float16)
                    for value, (way, part) in zip(arrived, chain)
                ]
            gate = sums
            moving[group] = [links.send(value, way) for value, (way, _) in zip(sums, chain)]

    def settle(part, *arrived):
        total = scores[0, :, part]
        for value in arrived:
            total = total + value.astype(jnp.float32)
        return total

    (low_ahead, high_back), (high_ahead, low_back) = moving
    parts = [settle(low, low_ahead, low_back), settle(high, high_ahead, high_back)]
    return jnp.concatenate(parts, axis=1)


def all_gather(links, own, side):
    chips = links.chips
    heads, rows, width = own.shape
    half = rows // 2
    deep = chips // 2
    gathered = jnp.zeros((2, chips) + own.shape, own.dtype)
    side = list(side)
    done = []
    batches = [(0, own)]
    ahead = back = own
    for far in range(1, deep):
        ahead = links.send(ahead, 1)
        back = links.send(back, -1)
        batches += [(chips - far, ahead), (far, back)]
        if side:
            (ahead, back), kept = lax.optimization_barrier(((ahead, back), side.pop(0)))
            done.append(kept)
    batches.append((deep, [links.send(ahead[:, :half], 1), links.send(back[:, half:], -1)]))
    for far, batch in batches:
        piece = jnp.concatenate(batch, axis=1) if far == deep else batch
        for core, value in enumerate((piece, links.swap(piece))):
            gathered = lax.dynamic_update_slice(gathered, value[None, None], (core, far, 0, 0, 0))
    return gathered, done + side


ROWS = 4
REACH = {1: (0, 1, 2, 3, 4, -1), 2: (0, 1, 2, 3, -2, -1, 4, 5)}


def taps_kernel(w_ref, near_ref, far_ref):
    size = w_ref.shape[1]
    zero = jnp.zeros((size, size), w_ref.dtype)
    for dilation, out_ref in ((1, near_ref), (2, far_ref)):
        for which in range(2):
            base = 9 * (2 * (dilation - 1) + which)
            for col in range(3):
                for slot, row in enumerate(REACH[dilation]):
                    pieces = []
                    for out_row in range(ROWS):
                        step, rest = divmod(row - out_row, dilation)
                        live = rest == 0 and -1 <= step <= 1
                        pieces.append(w_ref[base + 3 * (step + 1) + col] if live else zero)
                    out_ref[which, col, slot * size : (slot + 1) * size, :] = jnp.concatenate(
                        pieces, axis=1
                    )


def contact_kernel(
    index_ref, pf_ref, pair_ref, near_ref, far_ref, head_ref, o_ref, u_ref, v_ref, hid_ref
):
    blocks, _, residues = pf_ref.shape
    lanes = pair_ref.shape[1]
    size = lanes // ROWS
    half = lanes // 2
    bf16 = jnp.bfloat16
    position = lax.broadcasted_iota(jnp.int32, (residues, lanes), 0)
    lane_row = lax.broadcasted_iota(jnp.int32, (1, lanes), 1) // size

    def masked(m, values):
        row = index_ref[0] * o_ref.shape[0] + ROWS * (m - 2) + lane_row
        return jnp.where((row >= 0) & (row < residues), values, 0.0)

    def spread(ref, m, values, dilation):
        ref[1, m] = values.astype(bf16)
        left = jnp.where(position >= dilation, pltpu.roll(values, dilation, 0), 0.0)
        ref[0, m] = left.astype(bf16)
        right = jnp.where(
            position < residues - dilation, pltpu.roll(values, residues - dilation, 0), 0.0
        )
        ref[2, m] = right.astype(bf16)

    def conv(ref, m, w_ref, which, dilation):
        before = max(m - 1, 0)
        after = min(m + 1, blocks - 1)
        windows = []
        for col in range(3):
            low = ref[col, before, :, half:]
            high = ref[col, after, :, :half]
            if dilation == 1:
                lane = lax.broadcasted_iota(jnp.int32, low.shape, 1)
                edge = [jnp.where(lane < size, high, low)]
            else:
                edge = [low, high]
            windows += [ref[col, m]] + edge
        window = jnp.concatenate(windows, axis=1)
        weight = w_ref[which].reshape(window.shape[1], lanes)
        return jnp.dot(window, weight, preferred_element_type=jnp.float32)

    def start(m):
        hidden = lax.dot_general(
            pf_ref[m], pair_ref[...], (((0,), (0,)), ((), ())), preferred_element_type=jnp.float32
        )
        hid_ref[m] = hidden
        spread(u_ref, m, hidden, 1)

    for m in range(blocks):
        start(m)

    def first(m):
        inner = masked(m, jnp.maximum(conv(u_ref, m, near_ref, 0, 1), 0.0))
        spread(v_ref, m, inner, 1)

    for m in range(blocks):
        first(m)

    def second(m):
        hidden = masked(m, hid_ref[m] + conv(v_ref, m, near_ref, 1, 1))
        hid_ref[m] = hidden
        spread(u_ref, m, hidden, 2)

    for m in range(1, blocks - 1):
        second(m)

    def third(m):
        inner = masked(m, jnp.maximum(conv(u_ref, m, far_ref, 0, 2), 0.0))
        spread(v_ref, m, inner, 2)

    for m in range(1, blocks - 1):
        third(m)

    group = lax.broadcasted_iota(jnp.int32, (lanes, 128), 0) // size
    slot = lax.broadcasted_iota(jnp.int32, (lanes, 128), 1)

    def last(m, logits):
        hidden = hid_ref[m] + conv(v_ref, m, far_ref, 1, 2)
        weighed = hidden * head_ref[...]
        picks = jnp.where(slot == ROWS * (m - 2) + group, 1.0, 0.0).astype(bf16)
        for _ in range(3):
            coarse = weighed.astype(bf16)
            logits = logits + jnp.dot(coarse, picks, preferred_element_type=jnp.float32)
            weighed = weighed - coarse.astype(jnp.float32)
        return logits

    logits = jnp.zeros((residues, 128), jnp.float32)
    for m in range(2, blocks - 2):
        logits = last(m, logits)
    o_ref[...] = 1.0 / (1.0 + jnp.exp(-logits.T[: o_ref.shape[0]]))


def spread_taps(conv_weight):
    kinds, taps, size, _ = conv_weight.shape
    flipped = conv_weight.transpose(0, 1, 3, 2).reshape(kinds * taps, size, size)
    return pl.pallas_call(
        taps_kernel,
        out_shape=tuple(
            jax.ShapeDtypeStruct((2, 3, len(REACH[d]) * size, ROWS * size), conv_weight.dtype)
            for d in (1, 2)
        ),
        cost_estimate=cost(0, 6 << 20),
        name="spread_taps",
    )(flipped)


def window_kernel(index_ref, table_ref, p_ref, pf_ref, cols_ref, rows_ref):
    cores, chips, heads, rows, residues = p_ref.shape
    blocks, taken, _ = pf_ref.shape
    band = ROWS * blocks
    own_rows = band - 4 * ROWS
    first = index_ref[0] * own_rows - 2 * ROWS
    wide = cols_ref.shape[1] // (cores * heads)
    tall = rows_ref.shape[0] // (cores * heads)
    left = jnp.clip(lax.div(first, 128) * 128, 0, residues - wide)
    top = jnp.clip(lax.div(first, rows) * rows, 0, residues - tall)
    core = lax.rem(index_ref[0], 2)
    place = table_ref[lax.div(index_ref[0], 2)]
    lanes = pl.ds(pl.multiple_of(left, 128), wide)
    for ahead in range(chips):
        chip = ring_place(index_ref, table_ref, ahead)
        there = pl.ds(pl.multiple_of(chip * rows, rows), rows)
        for side in range(cores):
            for head in range(heads):
                slot = side * heads + head
                cols_ref[there, slot * wide : (slot + 1) * wide] = p_ref[side, ahead, head, :, lanes]
    for step in range(tall // rows):
        ahead = lax.rem(table_ref[lax.div(top, rows) + step] - place + chips, chips)
        for side in range(cores):
            for head in range(heads):
                start = (side * heads + head) * tall + step * rows
                rows_ref[start : start + rows, :] = p_ref[side, ahead, head]

    def picks(extent, base, out_rows, start):
        count = cores * heads * extent
        at = lax.broadcasted_iota(jnp.int32, (1, count), 1)
        slot = lax.div(at, extent)
        side = lax.div(slot, heads)
        head = lax.rem(side + core, 2) * heads + slot - side * heads
        have = head * 2048 + base + at - slot * extent
        out = start + lax.broadcasted_iota(jnp.int32, (out_rows, 1), 0)
        block = lax.div(out, taken)
        rest = out - block * taken
        head = lax.div(rest, ROWS)
        row = first + ROWS * block + rest - head * ROWS
        want = jnp.where((row >= 0) & (row < residues), head * 2048 + row, -1)
        return jnp.where(want == have, 1.0, 0.0).astype(jnp.bfloat16)

    step = 3 if blocks % 3 == 0 else 1
    for block in range(0, blocks, step):
        by_col = lax.dot_general(
            picks(wide, left, step * taken, block * taken),
            cols_ref[...],
            (((1,), (1,)), ((), ())),
            preferred_element_type=jnp.float32,
        )
        by_row = jnp.dot(
            picks(tall, top, step * taken, block * taken),
            rows_ref[...],
            preferred_element_type=jnp.float32,
        )
        both = ((by_col + by_row) * (residues * 0.5)).astype(jnp.bfloat16)
        pf_ref[block : block + step] = both.reshape(step, taken, residues)


def contact_head(links, probs, pair_weight, taps, head_weight):
    cores, chips, heads, rows, residues = probs.shape
    own_rows = residues // links.devices
    blocks = own_rows // ROWS + 4
    count = cores * heads
    wide = min(256, residues)
    tall = max(2 * rows, 64)
    smem = pl.BlockSpec(memory_space=pltpu.SMEM)
    vmem = pl.BlockSpec(memory_space=pltpu.VMEM)
    pair_features = pl.pallas_call(
        window_kernel,
        out_shape=jax.ShapeDtypeStruct((blocks, ROWS * count, residues), jnp.bfloat16),
        in_specs=[smem, smem, vmem],
        out_specs=vmem,
        scratch_shapes=[
            pltpu.VMEM((residues, count * wide), jnp.bfloat16),
            pltpu.VMEM((count * tall, residues), jnp.bfloat16),
        ],
        compiler_params=pltpu.CompilerParams(vmem_limit_bytes=40 << 20),
        cost_estimate=cost(2 * blocks * ROWS * count**2 * residues * (wide + tall), 2 * probs.size),
        name="pair_window",
    )(links.index, links.table, probs)
    return contact_call(links.index, pair_features, pair_weight, taps, head_weight, own_rows)


def contact_call(index, pair_features, pair_weight, taps, head_weight, own_rows):
    blocks, _, residues = pair_features.shape
    channels = pair_weight.shape[0]
    same = jnp.eye(ROWS, dtype=pair_weight.dtype)
    pair = (pair_weight.T[:, None, None, :] * same[None, :, :, None]).reshape(-1, ROWS * channels)
    head = jnp.tile(head_weight, ROWS)[None]
    lanes = ROWS * channels
    vmem = pl.BlockSpec(memory_space=pltpu.VMEM)
    work = 2 * residues * lanes * lanes * (13 * blocks + 17 * (blocks - 2))
    return pl.pallas_call(
        contact_kernel,
        out_shape=jax.ShapeDtypeStruct((own_rows, residues), jnp.float32),
        in_specs=[pl.BlockSpec(memory_space=pltpu.SMEM)] + [vmem] * 5,
        out_specs=vmem,
        scratch_shapes=[
            pltpu.VMEM((3, blocks, residues, lanes), jnp.bfloat16),
            pltpu.VMEM((3, blocks, residues, lanes), jnp.bfloat16),
            pltpu.VMEM((blocks, residues, lanes), jnp.float32),
        ],
        compiler_params=pltpu.CompilerParams(vmem_limit_bytes=48 << 20),
        cost_estimate=cost(work // 4, 4 << 20),
        name="contact_head",
    )(index, pair_features, pair, taps[0], taps[1], head)


def local(alignment, depth_count, qkv_weight, pair_weight, conv_weight, head_weight):
    seqs, residues, features = alignment.shape
    head_count = pair_weight.shape[1]
    size = features // head_count
    links = Links()
    sent, own, normed = projections(alignment, qkv_weight, links.index, depth_count, head_count)
    other = links.swap(sent)
    scores = scores_of(own, other, links.index, links.table, depth_count, size)
    summed = reduce_scatter(links, scores)
    probabilities = jax.nn.softmax(summed * (1.0 / LINK_SCALE), axis=-1).astype(jnp.bfloat16)
    probabilities, normed, conv_weight = lax.optimization_barrier(
        (probabilities, normed, conv_weight)
    )
    values = value_projection(normed, qkv_weight, head_count)
    gathered, (values, taps) = all_gather(links, probabilities, (values, spread_taps(conv_weight)))
    row_mix = row_mix_of(gathered, values, links.index, links.table, seqs, head_count)
    contacts = contact_head(links, gathered, pair_weight, taps, head_weight)
    return (row_mix, contacts)


def solution(mesh):
    return jax.shard_map(
        local,
        mesh=mesh,
        in_specs=(P(("grp", "seq"), None, None), P("grp"), P(), P(), P(), P()),
        out_specs=(P(("grp", "seq"), None, None), P(("grp", "seq"), None)),
        check_vma=False,
    )
```

```python
import functools

import jax
import jax.numpy as jnp
from jax import lax
from jax.experimental import pallas as pl
from jax.experimental.pallas import tpu as pltpu
from jax.sharding import PartitionSpec as P

EPSILON = 1e-05
LINK_SCALE = 2.0**-7


def grid_of(chips):
    width = 1
    while (2 * width) ** 2 <= chips:
        width *= 2
    return chips // width, width


def ring_of(chips):
    tall, wide = grid_of(chips)
    if tall % 2 or wide < 2:
        return list(range(chips))
    ring = [0]
    for row in range(tall):
        columns = range(1, wide) if row % 2 == 0 else range(wide - 1, 0, -1)
        ring += [row * wide + column for column in columns]
    return ring + [row * wide for row in range(tall - 1, 0, -1)]


def head_major(values, seqs, rows, size):
    out = []
    for head in range(values.shape[1] // size):
        pieces = [
            values[seq * rows : (seq + 1) * rows, head * size : (head + 1) * size]
            for seq in range(seqs)
        ]
        out.append(jnp.concatenate(pieces, axis=1))
    return out


def ring_place(index_ref, table_ref, ahead):
    chips = table_ref.shape[0] // 2
    place = table_ref[lax.div(index_ref[0], 2)]
    return table_ref[chips + lax.rem(place + ahead, chips)]


def rows_here(ref_rows):
    return pl.ds(pl.multiple_of(pl.program_id(0) * ref_rows, ref_rows), ref_rows)


def norm_send_kernel(index_ref, depth_ref, x_ref, wq_ref, wk_ref, normed_ref, qk_ref):
    seqs, rows, width = x_ref.shape
    values = x_ref[...].reshape(seqs * rows, width).astype(jnp.float32)
    average = jnp.mean(values, axis=-1, keepdims=True)
    centered = values - average
    variance = jnp.mean(centered * centered, axis=-1, keepdims=True)
    normed = (centered * lax.rsqrt(variance + EPSILON)).astype(jnp.bfloat16)
    normed_ref[:, rows_here(rows), :] = normed.reshape(seqs, rows, width)
    project(index_ref, depth_ref, normed, wq_ref, wk_ref, qk_ref, seqs, rows)


def own_kernel(rows, index_ref, depth_ref, normed_ref, wq_ref, wk_ref, qk_ref):
    seqs, _, width = normed_ref.shape
    normed = normed_ref[:, rows_here(rows), :].reshape(seqs * rows, width)
    project(index_ref, depth_ref, normed, wq_ref, wk_ref, qk_ref, seqs, rows)


def project(index_ref, depth_ref, normed, wq_ref, wk_ref, qk_ref, seqs, rows):
    size = qk_ref.shape[3] // seqs
    here = rows_here(rows)
    weight = jnp.concatenate([wq_ref[...], wk_ref[...]], axis=1)
    both = jnp.dot(normed, weight, preferred_element_type=jnp.float32).astype(jnp.bfloat16)
    q, k = both[:, : weight.shape[1] // 2], both[:, weight.shape[1] // 2 :]
    for head, block in enumerate(head_major(q, seqs, rows, size)):
        lane = lax.broadcasted_iota(jnp.int32, block.shape, 1)
        in_use = (depth_ref[0] - index_ref[0] * seqs) * size
        qk_ref[0, head, here, :] = jnp.where(lane < in_use, block, jnp.zeros_like(block))
    for head, block in enumerate(head_major(k, seqs, rows, size)):
        qk_ref[1, head, here, :] = block


def value_kernel(rows, normed_ref, w_ref, v_ref):
    seqs, _, width = normed_ref.shape
    size = v_ref.shape[2] // seqs
    here = rows_here(rows)
    normed = normed_ref[:, here, :].reshape(seqs * rows, width)
    v = jnp.dot(normed, w_ref[...], preferred_element_type=jnp.float32).astype(jnp.bfloat16)
    for head, block in enumerate(head_major(v, seqs, rows, size)):
        v_ref[head, here, :] = block


def score_kernel(size, index_ref, table_ref, depth_ref, own_ref, other_ref, s_ref):
    chips, _, rows, residues = s_ref.shape
    here = pl.program_id(0)
    depth = jnp.full((1, residues), depth_ref[0], jnp.int32).astype(jnp.float32)
    scale = size**-0.5 / jnp.sqrt(depth) * LINK_SCALE
    places = [
        pl.ds(pl.multiple_of(ring_place(index_ref, table_ref, ahead) * rows, rows), rows)
        for ahead in range(chips)
    ]
    total = None
    for ref in (own_ref, other_ref):
        q = jnp.concatenate([ref[0, here, place, :] for place in places], axis=0)
        part = lax.dot_general(
            q, ref[1, here], (((1,), (1,)), ((), ())), preferred_element_type=jnp.float32
        )
        total = part if total is None else total + part
    total = total * scale
    s_ref[:, here] = total.reshape(chips, rows, total.shape[1])


def mix_kernel(index_ref, table_ref, p_ref, v_ref, o_ref):
    seqs = o_ref.shape[0]
    size = v_ref.shape[2] // seqs
    _, chips, heads, rows, residues = p_ref.shape
    pairs = heads // 2
    step = pl.program_id(0)
    side = lax.div(step, pairs)
    first = 2 * lax.rem(step, pairs)
    start = lax.rem(index_ref[0] + side, 2) * heads + first
    mixed = []
    for head in range(2):
        probs = p_ref[side, :, first + head].reshape(chips * rows, residues)
        mixed.append(
            jnp.dot(probs, v_ref[start + head], preferred_element_type=jnp.float32).astype(
                jnp.bfloat16
            )
        )
    places = [
        pl.ds(pl.multiple_of(ring_place(index_ref, table_ref, ahead) * rows, rows), rows)
        for ahead in range(chips)
    ]
    for seq in range(seqs):
        joined = jnp.concatenate(
            [block[:, seq * size : (seq + 1) * size] for block in mixed], axis=1
        )
        for ahead, place in enumerate(places):
            o_ref[seq, place, :] = joined[ahead * rows : (ahead + 1) * rows]


def cost(flops, moved):
    return pl.CostEstimate(flops=int(flops), bytes_accessed=int(moved), transcendentals=0)


def projections(alignment, qkv_weight, index, depth_count, head_count):
    seqs, residues, features = alignment.shape
    heads = head_count // 2
    size = features // head_count
    rows = 256 if residues % 256 == 0 else residues
    cols = heads * size
    steps = residues // rows
    bf16 = jnp.bfloat16
    x_spec = pl.BlockSpec((seqs, rows, features), lambda i, *_: (0, i, 0))
    vmem = pl.BlockSpec(memory_space=pltpu.VMEM)
    qk_shape = jax.ShapeDtypeStruct((2, heads, residues, seqs * size), bf16)
    params = pltpu.CompilerParams(vmem_limit_bytes=48 << 20)

    def weight_specs(pick):
        return [
            pl.BlockSpec((features, cols), lambda i, index, _: (0, pick(lax.rem(index[0], 2)))),
            pl.BlockSpec((features, cols), lambda i, index, _: (0, 2 + pick(lax.rem(index[0], 2)))),
        ]

    flops = 4 * seqs * residues * features * cols
    moved = 2 * (seqs * residues * features + 2 * features * cols + 2 * seqs * residues * cols)
    normed, sent = pl.pallas_call(
        norm_send_kernel,
        out_shape=(jax.ShapeDtypeStruct(alignment.shape, bf16), qk_shape),
        grid_spec=pltpu.PrefetchScalarGridSpec(
            num_scalar_prefetch=2,
            grid=(steps,),
            in_specs=[x_spec] + weight_specs(lambda half: 1 - half),
            out_specs=[vmem, vmem],
        ),
        compiler_params=params,
        cost_estimate=cost(flops, moved + 2 * alignment.size),
        name="norm_send",
    )(index, depth_count, alignment, qkv_weight, qkv_weight)
    own = pl.pallas_call(
        functools.partial(own_kernel, rows),
        out_shape=qk_shape,
        grid_spec=pltpu.PrefetchScalarGridSpec(
            num_scalar_prefetch=2,
            grid=(steps,),
            in_specs=[vmem] + weight_specs(lambda half: half),
            out_specs=vmem,
        ),
        compiler_params=params,
        cost_estimate=cost(flops, moved),
        name="own_project",
    )(index, depth_count, normed, qkv_weight, qkv_weight)
    return sent, own, normed


def value_projection(normed, qkv_weight, head_count):
    seqs, residues, features = normed.shape
    size = features // head_count
    rows = 256 if residues % 256 == 0 else residues
    steps = residues // rows
    flops = 2 * seqs * residues * features * features
    moved = 2 * (2 * seqs * residues * features + features * features)
    bf16 = jnp.bfloat16
    params = pltpu.CompilerParams(vmem_limit_bytes=48 << 20)
    return pl.pallas_call(
        functools.partial(value_kernel, rows),
        out_shape=jax.ShapeDtypeStruct((head_count, residues, seqs * size), bf16),
        grid=(steps,),
        in_specs=[
            pl.BlockSpec(memory_space=pltpu.VMEM),
            pl.BlockSpec((features, features), lambda i: (0, 2)),
        ],
        out_specs=pl.BlockSpec(memory_space=pltpu.VMEM),
        compiler_params=params,
        cost_estimate=cost(flops, moved),
        name="value_project",
    )(normed, qkv_weight)


def scores_of(own, other, index, table, depth_count, size):
    _, heads, residues, inner = own.shape
    chips = table.shape[0] // 2
    rows = residues // chips
    spec = pl.BlockSpec(memory_space=pltpu.VMEM)
    return pl.pallas_call(
        functools.partial(score_kernel, size),
        out_shape=jax.ShapeDtypeStruct((chips, heads, rows, residues), jnp.float32),
        grid_spec=pltpu.PrefetchScalarGridSpec(
            num_scalar_prefetch=3,
            grid=(heads,),
            in_specs=[spec, spec],
            out_specs=spec,
        ),
        compiler_params=pltpu.CompilerParams(vmem_limit_bytes=32 << 20),
        cost_estimate=cost(4 * heads * residues * residues * inner, 4 * own.size + 4 * heads * residues**2),
        name="scores",
    )(index, table, depth_count, own, other)


def row_mix_of(probs, values, index, table, seqs, head_count):
    _, chips, heads, rows, residues = probs.shape
    inner = values.shape[2]
    size = inner // seqs
    pairs = heads // 2

    def pair_at(g, index):
        core = lax.rem(index[0] + lax.div(g, pairs), 2)
        return core * pairs + lax.rem(g, pairs)

    return pl.pallas_call(
        mix_kernel,
        out_shape=jax.ShapeDtypeStruct((seqs, residues, head_count * size), jnp.bfloat16),
        grid_spec=pltpu.PrefetchScalarGridSpec(
            num_scalar_prefetch=2,
            grid=(2 * pairs,),
            in_specs=[pl.BlockSpec(memory_space=pltpu.VMEM)] * 2,
            out_specs=pl.BlockSpec(
                (seqs, residues, 2 * size), lambda g, index, _: (0, 0, pair_at(g, index))
            ),
        ),
        compiler_params=pltpu.CompilerParams(vmem_limit_bytes=32 << 20),
        cost_estimate=cost(2 * probs.size * inner, 2 * (probs.size + 2 * values.size)),
        name="row_mix",
    )(index, table, probs, values)


class Links:
    def __init__(self):
        self.devices = lax.axis_size("seq")
        self.chips = self.devices // 2
        self.ring = ring_of(self.chips)
        places = [self.ring.index(chip) for chip in range(self.chips)]
        self.table = jnp.asarray(places + self.ring, jnp.int32)
        self.index = lax.axis_index("seq").astype(jnp.int32).reshape(1)

    def send(self, value, ahead):
        pairs = []
        for place, chip in enumerate(self.ring):
            target = self.ring[(place + ahead) % self.chips]
            pairs += [(2 * chip + core, 2 * target + core) for core in range(2)]
        return lax.ppermute(value, "seq", pairs)

    def swap(self, value):
        return lax.ppermute(value, "seq", [(i, i ^ 1) for i in range(self.devices)])


def reduce_scatter(links, scores):
    chips, _, rows, _ = scores.shape
    half = rows // 2
    low, high = slice(0, half), slice(half, rows)
    deep = chips // 2
    chains = [[(1, low), (-1, high)], [(1, high), (-1, low)]]

    def share(way, part, far):
        return scores[way * far % chips, :, part]

    moving = [None, None]
    gate = None
    for far in range(deep, 0, -1):
        for group in range(2):
            if group == 1 and far == deep:
                continue
            chain = chains[group]
            if moving[group] is None:
                sums = [share(way, part, far).astype(jnp.float16) for way, part in chain]
            else:
                arrived, _ = lax.optimization_barrier((moving[group], gate))
                sums = [
                    (value.astype(jnp.float32) + share(way, part, far)).astype(jnp.float16)
                    for value, (way, part) in zip(arrived, chain)
                ]
            gate = sums
            moving[group] = [links.send(value, way) for value, (way, _) in zip(sums, chain)]

    def settle(part, *arrived):
        total = scores[0, :, part]
        for value in arrived:
            total = total + value.astype(jnp.float32)
        return total

    (low_ahead, high_back), (high_ahead, low_back) = moving
    parts = [settle(low, low_ahead, low_back), settle(high, high_ahead, high_back)]
    return jnp.concatenate(parts, axis=1)


def all_gather(links, own, side):
    chips = links.chips
    heads, rows, width = own.shape
    half = rows // 2
    deep = chips // 2
    gathered = jnp.zeros((2, chips) + own.shape, own.dtype)
    side = list(side)
    done = []
    batches = [(0, own)]
    ahead = back = own
    for far in range(1, deep):
        ahead = links.send(ahead, 1)
        back = links.send(back, -1)
        batches += [(chips - far, ahead), (far, back)]
        if side:
            (ahead, back), kept = lax.optimization_barrier(((ahead, back), side.pop(0)))
            done.append(kept)
    batches.append((deep, [links.send(ahead[:, :half], 1), links.send(back[:, half:], -1)]))
    for far, batch in batches:
        piece = jnp.concatenate(batch, axis=1) if far == deep else batch
        for core, value in enumerate((piece, links.swap(piece))):
            gathered = lax.dynamic_update_slice(gathered, value[None, None], (core, far, 0, 0, 0))
    return gathered, done + side


ROWS = 4
REACH = {1: (0, 1, 2, 3, 4, -1), 2: (0, 1, 2, 3, -2, -1, 4, 5)}


def taps_kernel(w_ref, near_ref, far_ref):
    size = w_ref.shape[1]
    zero = jnp.zeros((size, size), w_ref.dtype)
    for dilation, out_ref in ((1, near_ref), (2, far_ref)):
        for which in range(2):
            base = 9 * (2 * (dilation - 1) + which)
            for col in range(3):
                for slot, row in enumerate(REACH[dilation]):
                    pieces = []
                    for out_row in range(ROWS):
                        step, rest = divmod(row - out_row, dilation)
                        live = rest == 0 and -1 <= step <= 1
                        pieces.append(w_ref[base + 3 * (step + 1) + col] if live else zero)
                    out_ref[which, col, slot * size : (slot + 1) * size, :] = jnp.concatenate(
                        pieces, axis=1
                    )


def contact_kernel(
    index_ref, pf_ref, pair_ref, near_ref, far_ref, head_ref, o_ref, u_ref, v_ref, hid_ref
):
    blocks, _, residues = pf_ref.shape
    lanes = pair_ref.shape[1]
    size = lanes // ROWS
    half = lanes // 2
    bf16 = jnp.bfloat16
    position = lax.broadcasted_iota(jnp.int32, (residues, lanes), 0)
    lane_row = lax.broadcasted_iota(jnp.int32, (1, lanes), 1) // size

    def masked(m, values):
        row = index_ref[0] * o_ref.shape[0] + ROWS * (m - 2) + lane_row
        return jnp.where((row >= 0) & (row < residues), values, 0.0)

    def spread(ref, m, values, dilation):
        ref[1, m] = values.astype(bf16)
        left = jnp.where(position >= dilation, pltpu.roll(values, dilation, 0), 0.0)
        ref[0, m] = left.astype(bf16)
        right = jnp.where(
            position < residues - dilation, pltpu.roll(values, residues - dilation, 0), 0.0
        )
        ref[2, m] = right.astype(bf16)

    def conv(ref, m, w_ref, which, dilation):
        before = max(m - 1, 0)
        after = min(m + 1, blocks - 1)
        windows = []
        for col in range(3):
            low = ref[col, before, :, half:]
            high = ref[col, after, :, :half]
            if dilation == 1:
                lane = lax.broadcasted_iota(jnp.int32, low.shape, 1)
                edge = [jnp.where(lane < size, high, low)]
            else:
                edge = [low, high]
            windows += [ref[col, m]] + edge
        window = jnp.concatenate(windows, axis=1)
        weight = w_ref[which].reshape(window.shape[1], lanes)
        return jnp.dot(window, weight, preferred_element_type=jnp.float32)

    def start(m):
        hidden = lax.dot_general(
            pf_ref[m], pair_ref[...], (((0,), (0,)), ((), ())), preferred_element_type=jnp.float32
        )
        hid_ref[m] = hidden
        spread(u_ref, m, hidden, 1)

    for m in range(blocks):
        start(m)

    def first(m):
        inner = masked(m, jnp.maximum(conv(u_ref, m, near_ref, 0, 1), 0.0))
        spread(v_ref, m, inner, 1)

    for m in range(blocks):
        first(m)

    def second(m):
        hidden = masked(m, hid_ref[m] + conv(v_ref, m, near_ref, 1, 1))
        hid_ref[m] = hidden
        spread(u_ref, m, hidden, 2)

    for m in range(1, blocks - 1):
        second(m)

    def third(m):
        inner = masked(m, jnp.maximum(conv(u_ref, m, far_ref, 0, 2), 0.0))
        spread(v_ref, m, inner, 2)

    for m in range(1, blocks - 1):
        third(m)

    group = lax.broadcasted_iota(jnp.int32, (lanes, 128), 0) // size
    slot = lax.broadcasted_iota(jnp.int32, (lanes, 128), 1)

    def last(m, logits):
        hidden = hid_ref[m] + conv(v_ref, m, far_ref, 1, 2)
        weighed = hidden * head_ref[...]
        picks = jnp.where(slot == ROWS * (m - 2) + group, 1.0, 0.0).astype(bf16)
        for _ in range(3):
            coarse = weighed.astype(bf16)
            logits = logits + jnp.dot(coarse, picks, preferred_element_type=jnp.float32)
            weighed = weighed - coarse.astype(jnp.float32)
        return logits

    logits = jnp.zeros((residues, 128), jnp.float32)
    for m in range(2, blocks - 2):
        logits = last(m, logits)
    o_ref[...] = 1.0 / (1.0 + jnp.exp(-logits.T[: o_ref.shape[0]]))


def spread_taps(conv_weight):
    kinds, taps, size, _ = conv_weight.shape
    flipped = conv_weight.transpose(0, 1, 3, 2).reshape(kinds * taps, size, size)
    return pl.pallas_call(
        taps_kernel,
        out_shape=tuple(
            jax.ShapeDtypeStruct((2, 3, len(REACH[d]) * size, ROWS * size), conv_weight.dtype)
            for d in (1, 2)
        ),
        cost_estimate=cost(0, 6 << 20),
        name="spread_taps",
    )(flipped)


def window_kernel(index_ref, table_ref, p_ref, pf_ref, cols_ref, rows_ref):
    cores, chips, heads, rows, residues = p_ref.shape
    blocks, taken, _ = pf_ref.shape
    band = ROWS * blocks
    own_rows = band - 4 * ROWS
    first = index_ref[0] * own_rows - 2 * ROWS
    wide = cols_ref.shape[1] // (cores * heads)
    tall = rows_ref.shape[0] // (cores * heads)
    left = jnp.clip(lax.div(first, 128) * 128, 0, residues - wide)
    top = jnp.clip(lax.div(first, rows) * rows, 0, residues - tall)
    core = lax.rem(index_ref[0], 2)
    place = table_ref[lax.div(index_ref[0], 2)]
    lanes = pl.ds(pl.multiple_of(left, 128), wide)
    for ahead in range(chips):
        chip = ring_place(index_ref, table_ref, ahead)
        there = pl.ds(pl.multiple_of(chip * rows, rows), rows)
        for side in range(cores):
            for head in range(heads):
                slot = side * heads + head
                cols_ref[there, slot * wide : (slot + 1) * wide] = p_ref[side, ahead, head, :, lanes]
    for step in range(tall // rows):
        ahead = lax.rem(table_ref[lax.div(top, rows) + step] - place + chips, chips)
        for side in range(cores):
            for head in range(heads):
                start = (side * heads + head) * tall + step * rows
                rows_ref[start : start + rows, :] = p_ref[side, ahead, head]

    def picks(extent, base, out_rows, start):
        count = cores * heads * extent
        at = lax.broadcasted_iota(jnp.int32, (1, count), 1)
        slot = lax.div(at, extent)
        side = lax.div(slot, heads)
        head = lax.rem(side + core, 2) * heads + slot - side * heads
        have = head * 2048 + base + at - slot * extent
        out = start + lax.broadcasted_iota(jnp.int32, (out_rows, 1), 0)
        block = lax.div(out, taken)
        rest = out - block * taken
        head = lax.div(rest, ROWS)
        row = first + ROWS * block + rest - head * ROWS
        want = jnp.where((row >= 0) & (row < residues), head * 2048 + row, -1)
        return jnp.where(want == have, 1.0, 0.0).astype(jnp.bfloat16)

    step = 3 if blocks % 3 == 0 else 1
    for block in range(0, blocks, step):
        by_col = lax.dot_general(
            picks(wide, left, step * taken, block * taken),
            cols_ref[...],
            (((1,), (1,)), ((), ())),
            preferred_element_type=jnp.float32,
        )
        by_row = jnp.dot(
            picks(tall, top, step * taken, block * taken),
            rows_ref[...],
            preferred_element_type=jnp.float32,
        )
        both = ((by_col + by_row) * (residues * 0.5)).astype(jnp.bfloat16)
        pf_ref[block : block + step] = both.reshape(step, taken, residues)


def contact_head(links, probs, pair_weight, taps, head_weight):
    cores, chips, heads, rows, residues = probs.shape
    own_rows = residues // links.devices
    blocks = own_rows // ROWS + 4
    count = cores * heads
    wide = min(256, residues)
    tall = max(2 * rows, 64)
    smem = pl.BlockSpec(memory_space=pltpu.SMEM)
    vmem = pl.BlockSpec(memory_space=pltpu.VMEM)
    pair_features = pl.pallas_call(
        window_kernel,
        out_shape=jax.ShapeDtypeStruct((blocks, ROWS * count, residues), jnp.bfloat16),
        in_specs=[smem, smem, vmem],
        out_specs=vmem,
        scratch_shapes=[
            pltpu.VMEM((residues, count * wide), jnp.bfloat16),
            pltpu.VMEM((count * tall, residues), jnp.bfloat16),
        ],
        compiler_params=pltpu.CompilerParams(vmem_limit_bytes=40 << 20),
        cost_estimate=cost(2 * blocks * ROWS * count**2 * residues * (wide + tall), 2 * probs.size),
        name="pair_window",
    )(links.index, links.table, probs)
    return contact_call(links.index, pair_features, pair_weight, taps, head_weight, own_rows)


def contact_call(index, pair_features, pair_weight, taps, head_weight, own_rows):
    blocks, _, residues = pair_features.shape
    channels = pair_weight.shape[0]
    same = jnp.eye(ROWS, dtype=pair_weight.dtype)
    pair = (pair_weight.T[:, None, None, :] * same[None, :, :, None]).reshape(-1, ROWS * channels)
    head = jnp.tile(head_weight, ROWS)[None]
    lanes = ROWS * channels
    vmem = pl.BlockSpec(memory_space=pltpu.VMEM)
    work = 2 * residues * lanes * lanes * (13 * blocks + 17 * (blocks - 2))
    return pl.pallas_call(
        contact_kernel,
        out_shape=jax.ShapeDtypeStruct((own_rows, residues), jnp.float32),
        in_specs=[pl.BlockSpec(memory_space=pltpu.SMEM)] + [vmem] * 5,
        out_specs=vmem,
        scratch_shapes=[
            pltpu.VMEM((3, blocks, residues, lanes), jnp.bfloat16),
            pltpu.VMEM((3, blocks, residues, lanes), jnp.bfloat16),
            pltpu.VMEM((blocks, residues, lanes), jnp.float32),
        ],
        compiler_params=pltpu.CompilerParams(vmem_limit_bytes=48 << 20),
        cost_estimate=cost(work // 4, 4 << 20),
        name="contact_head",
    )(index, pair_features, pair, taps[0], taps[1], head)


def local(alignment, depth_count, qkv_weight, pair_weight, conv_weight, head_weight):
    seqs, residues, features = alignment.shape
    head_count = pair_weight.shape[1]
    size = features // head_count
    links = Links()
    sent, own, normed = projections(alignment, qkv_weight, links.index, depth_count, head_count)
    other = links.swap(sent)
    scores = scores_of(own, other, links.index, links.table, depth_count, size)
    summed = reduce_scatter(links, scores)
    probabilities = jax.nn.softmax(summed * (1.0 / LINK_SCALE), axis=-1).astype(jnp.bfloat16)
    probabilities, normed, conv_weight = lax.optimization_barrier(
        (probabilities, normed, conv_weight)
    )
    values = value_projection(normed, qkv_weight, head_count)
    gathered, (values, taps) = all_gather(links, probabilities, (values, spread_taps(conv_weight)))
    row_mix = row_mix_of(gathered, values, links.index, links.table, seqs, head_count)
    contacts = contact_head(links, gathered, pair_weight, taps, head_weight)
    return (row_mix, contacts)


def solution(mesh):
    return jax.shard_map(
        local,
        mesh=mesh,
        in_specs=(P(("grp", "seq"), None, None), P("grp"), P(), P(), P(), P()),
        out_specs=(P(("grp", "seq"), None, None), P(("grp", "seq"), None)),
        check_vma=False,
    )
```

```python
import functools

import jax
import jax.numpy as jnp
from jax import lax
from jax.experimental import pallas as pl
from jax.experimental.pallas import tpu as pltpu
from jax.sharding import PartitionSpec as P

EPSILON = 1e-05
LINK_SCALE = 2.0**-7


def grid_of(chips):
    width = 1
    while (2 * width) ** 2 <= chips:
        width *= 2
    return chips // width, width


def ring_of(chips):
    tall, wide = grid_of(chips)
    if tall % 2 or wide < 2:
        return list(range(chips))
    ring = [0]
    for row in range(tall):
        columns = range(1, wide) if row % 2 == 0 else range(wide - 1, 0, -1)
        ring += [row * wide + column for column in columns]
    return ring + [row * wide for row in range(tall - 1, 0, -1)]


def head_major(values, seqs, rows, size):
    out = []
    for head in range(values.shape[1] // size):
        pieces = [
            values[seq * rows : (seq + 1) * rows, head * size : (head + 1) * size]
            for seq in range(seqs)
        ]
        out.append(jnp.concatenate(pieces, axis=1))
    return out


def ring_place(index_ref, table_ref, ahead):
    chips = table_ref.shape[0] // 2
    place = table_ref[lax.div(index_ref[0], 2)]
    return table_ref[chips + lax.rem(place + ahead, chips)]


def rows_here(ref_rows):
    return pl.ds(pl.multiple_of(pl.program_id(0) * ref_rows, ref_rows), ref_rows)


def norm_send_kernel(index_ref, depth_ref, x_ref, wq_ref, wk_ref, normed_ref, qk_ref):
    seqs, rows, width = x_ref.shape
    values = x_ref[...].reshape(seqs * rows, width).astype(jnp.float32)
    average = jnp.mean(values, axis=-1, keepdims=True)
    centered = values - average
    variance = jnp.mean(centered * centered, axis=-1, keepdims=True)
    normed = (centered * lax.rsqrt(variance + EPSILON)).astype(jnp.bfloat16)
    normed_ref[:, rows_here(rows), :] = normed.reshape(seqs, rows, width)
    project(index_ref, depth_ref, normed, wq_ref, wk_ref, qk_ref, seqs, rows)


def own_kernel(rows, index_ref, depth_ref, normed_ref, wq_ref, wk_ref, qk_ref):
    seqs, _, width = normed_ref.shape
    normed = normed_ref[:, rows_here(rows), :].reshape(seqs * rows, width)
    project(index_ref, depth_ref, normed, wq_ref, wk_ref, qk_ref, seqs, rows)


def project(index_ref, depth_ref, normed, wq_ref, wk_ref, qk_ref, seqs, rows):
    size = qk_ref.shape[3] // seqs
    here = rows_here(rows)
    weight = jnp.concatenate([wq_ref[...], wk_ref[...]], axis=1)
    both = jnp.dot(normed, weight, preferred_element_type=jnp.float32).astype(jnp.bfloat16)
    q, k = both[:, : weight.shape[1] // 2], both[:, weight.shape[1] // 2 :]
    for head, block in enumerate(head_major(q, seqs, rows, size)):
        lane = lax.broadcasted_iota(jnp.int32, block.shape, 1)
        in_use = (depth_ref[0] - index_ref[0] * seqs) * size
        qk_ref[0, head, here, :] = jnp.where(lane < in_use, block, jnp.zeros_like(block))
    for head, block in enumerate(head_major(k, seqs, rows, size)):
        qk_ref[1, head, here, :] = block


def value_kernel(rows, normed_ref, w_ref, v_ref):
    seqs, _, width = normed_ref.shape
    size = v_ref.shape[2] // seqs
    here = rows_here(rows)
    normed = normed_ref[:, here, :].reshape(seqs * rows, width)
    v = jnp.dot(normed, w_ref[...], preferred_element_type=jnp.float32).astype(jnp.bfloat16)
    for head, block in enumerate(head_major(v, seqs, rows, size)):
        v_ref[head, here, :] = block


def score_kernel(size, index_ref, table_ref, depth_ref, own_ref, other_ref, s_ref):
    chips, _, rows, residues = s_ref.shape
    here = pl.program_id(0)
    depth = jnp.full((1, residues), depth_ref[0], jnp.int32).astype(jnp.float32)
    scale = size**-0.5 / jnp.sqrt(depth) * LINK_SCALE
    places = [
        pl.ds(pl.multiple_of(ring_place(index_ref, table_ref, ahead) * rows, rows), rows)
        for ahead in range(chips)
    ]
    total = None
    for ref in (own_ref, other_ref):
        q = jnp.concatenate([ref[0, here, place, :] for place in places], axis=0)
        part = lax.dot_general(
            q, ref[1, here], (((1,), (1,)), ((), ())), preferred_element_type=jnp.float32
        )
        total = part if total is None else total + part
    total = total * scale
    s_ref[:, here] = total.reshape(chips, rows, total.shape[1])


def mix_kernel(index_ref, table_ref, p_ref, v_ref, o_ref):
    seqs = o_ref.shape[0]
    size = v_ref.shape[2] // seqs
    _, chips, heads, rows, residues = p_ref.shape
    pairs = heads // 2
    step = pl.program_id(0)
    side = lax.div(step, pairs)
    first = 2 * lax.rem(step, pairs)
    start = lax.rem(index_ref[0] + side, 2) * heads + first
    mixed = []
    for head in range(2):
        probs = p_ref[side, :, first + head].reshape(chips * rows, residues)
        mixed.append(
            jnp.dot(probs, v_ref[start + head], preferred_element_type=jnp.float32).astype(
                jnp.bfloat16
            )
        )
    places = [
        pl.ds(pl.multiple_of(ring_place(index_ref, table_ref, ahead) * rows, rows), rows)
        for ahead in range(chips)
    ]
    for seq in range(seqs):
        joined = jnp.concatenate(
            [block[:, seq * size : (seq + 1) * size] for block in mixed], axis=1
        )
        for ahead, place in enumerate(places):
            o_ref[seq, place, :] = joined[ahead * rows : (ahead + 1) * rows]


def cost(flops, moved):
    return pl.CostEstimate(flops=int(flops), bytes_accessed=int(moved), transcendentals=0)


def projections(alignment, qkv_weight, index, depth_count, head_count):
    seqs, residues, features = alignment.shape
    heads = head_count // 2
    size = features // head_count
    rows = 256 if residues % 256 == 0 else residues
    cols = heads * size
    steps = residues // rows
    bf16 = jnp.bfloat16
    x_spec = pl.BlockSpec((seqs, rows, features), lambda i, *_: (0, i, 0))
    vmem = pl.BlockSpec(memory_space=pltpu.VMEM)
    qk_shape = jax.ShapeDtypeStruct((2, heads, residues, seqs * size), bf16)
    params = pltpu.CompilerParams(vmem_limit_bytes=48 << 20)

    def weight_specs(pick):
        return [
            pl.BlockSpec((features, cols), lambda i, index, _: (0, pick(lax.rem(index[0], 2)))),
            pl.BlockSpec((features, cols), lambda i, index, _: (0, 2 + pick(lax.rem(index[0], 2)))),
        ]

    flops = 4 * seqs * residues * features * cols
    moved = 2 * (seqs * residues * features + 2 * features * cols + 2 * seqs * residues * cols)
    normed, sent = pl.pallas_call(
        norm_send_kernel,
        out_shape=(jax.ShapeDtypeStruct(alignment.shape, bf16), qk_shape),
        grid_spec=pltpu.PrefetchScalarGridSpec(
            num_scalar_prefetch=2,
            grid=(steps,),
            in_specs=[x_spec] + weight_specs(lambda half: 1 - half),
            out_specs=[vmem, vmem],
        ),
        compiler_params=params,
        cost_estimate=cost(flops, moved + 2 * alignment.size),
        name="norm_send",
    )(index, depth_count, alignment, qkv_weight, qkv_weight)
    own = pl.pallas_call(
        functools.partial(own_kernel, rows),
        out_shape=qk_shape,
        grid_spec=pltpu.PrefetchScalarGridSpec(
            num_scalar_prefetch=2,
            grid=(steps,),
            in_specs=[vmem] + weight_specs(lambda half: half),
            out_specs=vmem,
        ),
        compiler_params=params,
        cost_estimate=cost(flops, moved),
        name="own_project",
    )(index, depth_count, normed, qkv_weight, qkv_weight)
    return sent, own, normed


def value_projection(normed, qkv_weight, head_count):
    seqs, residues, features = normed.shape
    size = features // head_count
    rows = 256 if residues % 256 == 0 else residues
    steps = residues // rows
    flops = 2 * seqs * residues * features * features
    moved = 2 * (2 * seqs * residues * features + features * features)
    bf16 = jnp.bfloat16
    params = pltpu.CompilerParams(vmem_limit_bytes=48 << 20)
    return pl.pallas_call(
        functools.partial(value_kernel, rows),
        out_shape=jax.ShapeDtypeStruct((head_count, residues, seqs * size), bf16),
        grid=(steps,),
        in_specs=[
            pl.BlockSpec(memory_space=pltpu.VMEM),
            pl.BlockSpec((features, features), lambda i: (0, 2)),
        ],
        out_specs=pl.BlockSpec(memory_space=pltpu.VMEM),
        compiler_params=params,
        cost_estimate=cost(flops, moved),
        name="value_project",
    )(normed, qkv_weight)


def scores_of(own, other, index, table, depth_count, size):
    _, heads, residues, inner = own.shape
    chips = table.shape[0] // 2
    rows = residues // chips
    spec = pl.BlockSpec(memory_space=pltpu.VMEM)
    return pl.pallas_call(
        functools.partial(score_kernel, size),
        out_shape=jax.ShapeDtypeStruct((chips, heads, rows, residues), jnp.float32),
        grid_spec=pltpu.PrefetchScalarGridSpec(
            num_scalar_prefetch=3,
            grid=(heads,),
            in_specs=[spec, spec],
            out_specs=spec,
        ),
        compiler_params=pltpu.CompilerParams(vmem_limit_bytes=32 << 20),
        cost_estimate=cost(4 * heads * residues * residues * inner, 4 * own.size + 4 * heads * residues**2),
        name="scores",
    )(index, table, depth_count, own, other)


def row_mix_of(probs, values, index, table, seqs, head_count):
    _, chips, heads, rows, residues = probs.shape
    inner = values.shape[2]
    size = inner // seqs
    pairs = heads // 2

    def pair_at(g, index):
        core = lax.rem(index[0] + lax.div(g, pairs), 2)
        return core * pairs + lax.rem(g, pairs)

    return pl.pallas_call(
        mix_kernel,
        out_shape=jax.ShapeDtypeStruct((seqs, residues, head_count * size), jnp.bfloat16),
        grid_spec=pltpu.PrefetchScalarGridSpec(
            num_scalar_prefetch=2,
            grid=(2 * pairs,),
            in_specs=[pl.BlockSpec(memory_space=pltpu.VMEM)] * 2,
            out_specs=pl.BlockSpec(
                (seqs, residues, 2 * size), lambda g, index, _: (0, 0, pair_at(g, index))
            ),
        ),
        compiler_params=pltpu.CompilerParams(vmem_limit_bytes=32 << 20),
        cost_estimate=cost(2 * probs.size * inner, 2 * (probs.size + 2 * values.size)),
        name="row_mix",
    )(index, table, probs, values)


class Links:
    def __init__(self):
        self.devices = lax.axis_size("seq")
        self.chips = self.devices // 2
        self.ring = ring_of(self.chips)
        places = [self.ring.index(chip) for chip in range(self.chips)]
        self.table = jnp.asarray(places + self.ring, jnp.int32)
        self.index = lax.axis_index("seq").astype(jnp.int32).reshape(1)

    def send(self, value, ahead):
        pairs = []
        for place, chip in enumerate(self.ring):
            target = self.ring[(place + ahead) % self.chips]
            pairs += [(2 * chip + core, 2 * target + core) for core in range(2)]
        return lax.ppermute(value, "seq", pairs)

    def swap(self, value):
        return lax.ppermute(value, "seq", [(i, i ^ 1) for i in range(self.devices)])


def reduce_scatter(links, scores):
    chips, _, rows, _ = scores.shape
    half = rows // 2
    low, high = slice(0, half), slice(half, rows)
    deep = chips // 2
    chains = [[(1, low), (-1, high)], [(1, high), (-1, low)]]

    def share(way, part, far):
        return scores[way * far % chips, :, part]

    moving = [None, None]
    gate = None
    for far in range(deep, 0, -1):
        for group in range(2):
            if group == 1 and far == deep:
                continue
            chain = chains[group]
            if moving[group] is None:
                sums = [share(way, part, far).astype(jnp.float16) for way, part in chain]
            else:
                arrived, _ = lax.optimization_barrier((moving[group], gate))
                sums = [
                    (value.astype(jnp.float32) + share(way, part, far)).astype(jnp.float16)
                    for value, (way, part) in zip(arrived, chain)
                ]
            gate = sums
            moving[group] = [links.send(value, way) for value, (way, _) in zip(sums, chain)]

    def settle(part, *arrived):
        total = scores[0, :, part]
        for value in arrived:
            total = total + value.astype(jnp.float32)
        return total

    (low_ahead, high_back), (high_ahead, low_back) = moving
    parts = [settle(low, low_ahead, low_back), settle(high, high_ahead, high_back)]
    return jnp.concatenate(parts, axis=1)


def all_gather(links, own, side):
    chips = links.chips
    heads, rows, width = own.shape
    half = rows // 2
    deep = chips // 2
    gathered = jnp.zeros((2, chips) + own.shape, own.dtype)
    side = list(side)
    done = []
    batches = [(0, own)]
    ahead = back = own
    for far in range(1, deep):
        ahead = links.send(ahead, 1)
        back = links.send(back, -1)
        batches += [(chips - far, ahead), (far, back)]
        if side:
            (ahead, back), kept = lax.optimization_barrier(((ahead, back), side.pop(0)))
            done.append(kept)
    batches.append((deep, [links.send(ahead[:, :half], 1), links.send(back[:, half:], -1)]))
    for far, batch in batches:
        piece = jnp.concatenate(batch, axis=1) if far == deep else batch
        for core, value in enumerate((piece, links.swap(piece))):
            gathered = lax.dynamic_update_slice(gathered, value[None, None], (core, far, 0, 0, 0))
    return gathered, done + side


ROWS = 4
REACH = {1: (0, 1, 2, 3, 4, -1), 2: (0, 1, 2, 3, -2, -1, 4, 5)}


def taps_kernel(w_ref, near_ref, far_ref):
    size = w_ref.shape[1]
    zero = jnp.zeros((size, size), w_ref.dtype)
    for dilation, out_ref in ((1, near_ref), (2, far_ref)):
        for which in range(2):
            base = 9 * (2 * (dilation - 1) + which)
            for col in range(3):
                for slot, row in enumerate(REACH[dilation]):
                    pieces = []
                    for out_row in range(ROWS):
                        step, rest = divmod(row - out_row, dilation)
                        live = rest == 0 and -1 <= step <= 1
                        pieces.append(w_ref[base + 3 * (step + 1) + col] if live else zero)
                    out_ref[which, col, slot * size : (slot + 1) * size, :] = jnp.concatenate(
                        pieces, axis=1
                    )


def contact_kernel(
    index_ref, pf_ref, pair_ref, near_ref, far_ref, head_ref, o_ref, u_ref, v_ref, hid_ref
):
    blocks, _, residues = pf_ref.shape
    lanes = pair_ref.shape[1]
    size = lanes // ROWS
    half = lanes // 2
    bf16 = jnp.bfloat16
    position = lax.broadcasted_iota(jnp.int32, (residues, lanes), 0)
    lane_row = lax.broadcasted_iota(jnp.int32, (1, lanes), 1) // size

    def masked(m, values):
        if 2 <= m < blocks - 2:
            return values
        row = index_ref[0] * o_ref.shape[0] + ROWS * (m - 2) + lane_row
        return jnp.where((row >= 0) & (row < residues), values, 0.0)

    def spread(ref, m, values, dilation):
        ref[1, m] = values.astype(bf16)
        left = jnp.where(position >= dilation, pltpu.roll(values, dilation, 0), 0.0)
        ref[0, m] = left.astype(bf16)
        right = jnp.where(
            position < residues - dilation, pltpu.roll(values, residues - dilation, 0), 0.0
        )
        ref[2, m] = right.astype(bf16)

    def conv(ref, m, w_ref, which, dilation):
        before = max(m - 1, 0)
        after = min(m + 1, blocks - 1)
        windows = []
        for col in range(3):
            low = ref[col, before, :, half:]
            high = ref[col, after, :, :half]
            if dilation == 1:
                lane = lax.broadcasted_iota(jnp.int32, low.shape, 1)
                edge = [jnp.where(lane < size, high, low)]
            else:
                edge = [low, high]
            windows += [ref[col, m]] + edge
        window = jnp.concatenate(windows, axis=1)
        weight = w_ref[which].reshape(window.shape[1], lanes)
        return jnp.dot(window, weight, preferred_element_type=jnp.float32)

    def start(m):
        hidden = lax.dot_general(
            pf_ref[m], pair_ref[...], (((0,), (0,)), ((), ())), preferred_element_type=jnp.float32
        )
        hid_ref[m] = hidden
        spread(u_ref, m, hidden, 1)

    for m in range(blocks):
        start(m)

    def first(m):
        inner = masked(m, jnp.maximum(conv(u_ref, m, near_ref, 0, 1), 0.0))
        spread(v_ref, m, inner, 1)

    for m in range(blocks):
        first(m)

    def second(m):
        hidden = masked(m, hid_ref[m] + conv(v_ref, m, near_ref, 1, 1))
        hid_ref[m] = hidden
        spread(u_ref, m, hidden, 2)

    for m in range(1, blocks - 1):
        second(m)

    def third(m):
        inner = masked(m, jnp.maximum(conv(u_ref, m, far_ref, 0, 2), 0.0))
        spread(v_ref, m, inner, 2)

    for m in range(1, blocks - 1):
        third(m)

    group = lax.broadcasted_iota(jnp.int32, (lanes, 128), 0) // size
    slot = lax.broadcasted_iota(jnp.int32, (lanes, 128), 1)

    def last(m, logits):
        hidden = hid_ref[m] + conv(v_ref, m, far_ref, 1, 2)
        weighed = hidden * head_ref[...]
        picks = jnp.where(slot == ROWS * (m - 2) + group, 1.0, 0.0).astype(bf16)
        for _ in range(3):
            coarse = weighed.astype(bf16)
            logits = logits + jnp.dot(coarse, picks, preferred_element_type=jnp.float32)
            weighed = weighed - coarse.astype(jnp.float32)
        return logits

    logits = jnp.zeros((residues, 128), jnp.float32)
    for m in range(2, blocks - 2):
        logits = last(m, logits)
    o_ref[...] = 1.0 / (1.0 + jnp.exp(-logits.T[: o_ref.shape[0]]))


def spread_taps(conv_weight):
    kinds, taps, size, _ = conv_weight.shape
    flipped = conv_weight.transpose(0, 1, 3, 2).reshape(kinds * taps, size, size)
    return pl.pallas_call(
        taps_kernel,
        out_shape=tuple(
            jax.ShapeDtypeStruct((2, 3, len(REACH[d]) * size, ROWS * size), conv_weight.dtype)
            for d in (1, 2)
        ),
        cost_estimate=cost(0, 6 << 20),
        name="spread_taps",
    )(flipped)


def window_kernel(index_ref, table_ref, p_ref, pf_ref, cols_ref, rows_ref):
    cores, chips, heads, rows, residues = p_ref.shape
    blocks, taken, _ = pf_ref.shape
    band = ROWS * blocks
    own_rows = band - 4 * ROWS
    first = index_ref[0] * own_rows - 2 * ROWS
    wide = cols_ref.shape[1] // (cores * heads)
    tall = rows_ref.shape[0] // (cores * heads)
    left = jnp.clip(lax.div(first, 128) * 128, 0, residues - wide)
    top = jnp.clip(lax.div(first, rows) * rows, 0, residues - tall)
    core = lax.rem(index_ref[0], 2)
    place = table_ref[lax.div(index_ref[0], 2)]
    lanes = pl.ds(pl.multiple_of(left, 128), wide)
    for ahead in range(chips):
        chip = ring_place(index_ref, table_ref, ahead)
        there = pl.ds(pl.multiple_of(chip * rows, rows), rows)
        for side in range(cores):
            for head in range(heads):
                slot = side * heads + head
                cols_ref[there, slot * wide : (slot + 1) * wide] = p_ref[side, ahead, head, :, lanes]
    for step in range(tall // rows):
        ahead = lax.rem(table_ref[lax.div(top, rows) + step] - place + chips, chips)
        for side in range(cores):
            for head in range(heads):
                start = (side * heads + head) * tall + step * rows
                rows_ref[start : start + rows, :] = p_ref[side, ahead, head]

    def picks(extent, base, out_rows, start):
        count = cores * heads * extent
        at = lax.broadcasted_iota(jnp.int32, (1, count), 1)
        slot = lax.div(at, extent)
        side = lax.div(slot, heads)
        head = lax.rem(side + core, 2) * heads + slot - side * heads
        have = head * 2048 + base + at - slot * extent
        out = start + lax.broadcasted_iota(jnp.int32, (out_rows, 1), 0)
        block = lax.div(out, taken)
        rest = out - block * taken
        head = lax.div(rest, ROWS)
        row = first + ROWS * block + rest - head * ROWS
        want = jnp.where((row >= 0) & (row < residues), head * 2048 + row, -1)
        return jnp.where(want == have, 1.0, 0.0).astype(jnp.bfloat16)

    step = blocks
    for block in range(0, blocks, step):
        by_col = lax.dot_general(
            picks(wide, left, step * taken, block * taken),
            cols_ref[...],
            (((1,), (1,)), ((), ())),
            preferred_element_type=jnp.float32,
        )
        by_row = jnp.dot(
            picks(tall, top, step * taken, block * taken),
            rows_ref[...],
            preferred_element_type=jnp.float32,
        )
        both = ((by_col + by_row) * (residues * 0.5)).astype(jnp.bfloat16)
        pf_ref[block : block + step] = both.reshape(step, taken, residues)


def contact_head(links, probs, pair_weight, taps, head_weight):
    cores, chips, heads, rows, residues = probs.shape
    own_rows = residues // links.devices
    blocks = own_rows // ROWS + 4
    count = cores * heads
    wide = min(256, residues)
    tall = max(2 * rows, 64)
    smem = pl.BlockSpec(memory_space=pltpu.SMEM)
    vmem = pl.BlockSpec(memory_space=pltpu.VMEM)
    pair_features = pl.pallas_call(
        window_kernel,
        out_shape=jax.ShapeDtypeStruct((blocks, ROWS * count, residues), jnp.bfloat16),
        in_specs=[smem, smem, vmem],
        out_specs=vmem,
        scratch_shapes=[
            pltpu.VMEM((residues, count * wide), jnp.bfloat16),
            pltpu.VMEM((count * tall, residues), jnp.bfloat16),
        ],
        compiler_params=pltpu.CompilerParams(vmem_limit_bytes=40 << 20),
        cost_estimate=cost(2 * blocks * ROWS * count**2 * residues * (wide + tall), 2 * probs.size),
        name="pair_window",
    )(links.index, links.table, probs)
    return contact_call(links.index, pair_features, pair_weight, taps, head_weight, own_rows)


def contact_call(index, pair_features, pair_weight, taps, head_weight, own_rows):
    blocks, _, residues = pair_features.shape
    channels = pair_weight.shape[0]
    same = jnp.eye(ROWS, dtype=pair_weight.dtype)
    pair = (pair_weight.T[:, None, None, :] * same[None, :, :, None]).reshape(-1, ROWS * channels)
    head = jnp.tile(head_weight, ROWS)[None]
    lanes = ROWS * channels
    vmem = pl.BlockSpec(memory_space=pltpu.VMEM)
    work = 2 * residues * lanes * lanes * (13 * blocks + 17 * (blocks - 2))
    return pl.pallas_call(
        contact_kernel,
        out_shape=jax.ShapeDtypeStruct((own_rows, residues), jnp.float32),
        in_specs=[pl.BlockSpec(memory_space=pltpu.SMEM)] + [vmem] * 5,
        out_specs=vmem,
        scratch_shapes=[
            pltpu.VMEM((3, blocks, residues, lanes), jnp.bfloat16),
            pltpu.VMEM((3, blocks, residues, lanes), jnp.bfloat16),
            pltpu.VMEM((blocks, residues, lanes), jnp.float32),
        ],
        compiler_params=pltpu.CompilerParams(vmem_limit_bytes=48 << 20),
        cost_estimate=cost(work // 4, 4 << 20),
        name="contact_head",
    )(index, pair_features, pair, taps[0], taps[1], head)


def local(alignment, depth_count, qkv_weight, pair_weight, conv_weight, head_weight):
    seqs, residues, features = alignment.shape
    head_count = pair_weight.shape[1]
    size = features // head_count
    links = Links()
    sent, own, normed = projections(alignment, qkv_weight, links.index, depth_count, head_count)
    other = links.swap(sent)
    scores = scores_of(own, other, links.index, links.table, depth_count, size)
    summed = reduce_scatter(links, scores)
    probabilities = jax.nn.softmax(summed * (1.0 / LINK_SCALE), axis=-1).astype(jnp.bfloat16)
    probabilities, normed, conv_weight = lax.optimization_barrier(
        (probabilities, normed, conv_weight)
    )
    values = value_projection(normed, qkv_weight, head_count)
    gathered, (values, taps) = all_gather(links, probabilities, (values, spread_taps(conv_weight)))
    row_mix = row_mix_of(gathered, values, links.index, links.table, seqs, head_count)
    contacts = contact_head(links, gathered, pair_weight, taps, head_weight)
    return (row_mix, contacts)


def solution(mesh):
    return jax.shard_map(
        local,
        mesh=mesh,
        in_specs=(P(("grp", "seq"), None, None), P("grp"), P(), P(), P(), P()),
        out_specs=(P(("grp", "seq"), None, None), P(("grp", "seq"), None)),
        check_vma=False,
    )
```

```python
import functools

import jax
import jax.numpy as jnp
from jax import lax
from jax.experimental import pallas as pl
from jax.experimental.pallas import tpu as pltpu
from jax.sharding import PartitionSpec as P

EPSILON = 1e-05
LINK_SCALE = 2.0**-7


def grid_of(chips):
    width = 1
    while (2 * width) ** 2 <= chips:
        width *= 2
    return chips // width, width


def ring_of(chips):
    tall, wide = grid_of(chips)
    if tall % 2 or wide < 2:
        return list(range(chips))
    ring = [0]
    for row in range(tall):
        columns = range(1, wide) if row % 2 == 0 else range(wide - 1, 0, -1)
        ring += [row * wide + column for column in columns]
    return ring + [row * wide for row in range(tall - 1, 0, -1)]


def head_major(values, seqs, rows, size):
    out = []
    for head in range(values.shape[1] // size):
        pieces = [
            values[seq * rows : (seq + 1) * rows, head * size : (head + 1) * size]
            for seq in range(seqs)
        ]
        out.append(jnp.concatenate(pieces, axis=1))
    return out


def ring_place(index_ref, table_ref, ahead):
    chips = table_ref.shape[0] // 2
    place = table_ref[lax.div(index_ref[0], 2)]
    return table_ref[chips + lax.rem(place + ahead, chips)]


def rows_here(ref_rows):
    return pl.ds(pl.multiple_of(pl.program_id(0) * ref_rows, ref_rows), ref_rows)


def norm_send_kernel(index_ref, depth_ref, x_ref, wq_ref, wk_ref, normed_ref, qk_ref):
    seqs, rows, width = x_ref.shape
    values = x_ref[...].reshape(seqs * rows, width).astype(jnp.float32)
    average = jnp.mean(values, axis=-1, keepdims=True)
    centered = values - average
    variance = jnp.mean(centered * centered, axis=-1, keepdims=True)
    normed = (centered * lax.rsqrt(variance + EPSILON)).astype(jnp.bfloat16)
    normed_ref[:, rows_here(rows), :] = normed.reshape(seqs, rows, width)
    project(index_ref, depth_ref, normed, wq_ref, wk_ref, qk_ref, seqs, rows)


def own_kernel(rows, index_ref, depth_ref, normed_ref, wq_ref, wk_ref, qk_ref):
    seqs, _, width = normed_ref.shape
    normed = normed_ref[:, rows_here(rows), :].reshape(seqs * rows, width)
    project(index_ref, depth_ref, normed, wq_ref, wk_ref, qk_ref, seqs, rows)


def project(index_ref, depth_ref, normed, wq_ref, wk_ref, qk_ref, seqs, rows):
    size = qk_ref.shape[3] // seqs
    here = rows_here(rows)
    weight = jnp.concatenate([wq_ref[...], wk_ref[...]], axis=1)
    both = jnp.dot(normed, weight, preferred_element_type=jnp.float32).astype(jnp.bfloat16)
    q, k = both[:, : weight.shape[1] // 2], both[:, weight.shape[1] // 2 :]
    for head, block in enumerate(head_major(q, seqs, rows, size)):
        lane = lax.broadcasted_iota(jnp.int32, block.shape, 1)
        in_use = (depth_ref[0] - index_ref[0] * seqs) * size
        qk_ref[0, head, here, :] = jnp.where(lane < in_use, block, jnp.zeros_like(block))
    for head, block in enumerate(head_major(k, seqs, rows, size)):
        qk_ref[1, head, here, :] = block


def value_kernel(rows, normed_ref, w_ref, v_ref):
    seqs, _, width = normed_ref.shape
    size = v_ref.shape[2] // seqs
    here = rows_here(rows)
    normed = normed_ref[:, here, :].reshape(seqs * rows, width)
    v = jnp.dot(normed, w_ref[...], preferred_element_type=jnp.float32).astype(jnp.bfloat16)
    for head, block in enumerate(head_major(v, seqs, rows, size)):
        v_ref[head, here, :] = block


def score_kernel(size, index_ref, table_ref, depth_ref, own_ref, other_ref, s_ref):
    chips, _, rows, residues = s_ref.shape
    here = pl.program_id(0)
    depth = jnp.full((1, residues), depth_ref[0], jnp.int32).astype(jnp.float32)
    scale = size**-0.5 / jnp.sqrt(depth) * LINK_SCALE
    places = [
        pl.ds(pl.multiple_of(ring_place(index_ref, table_ref, ahead) * rows, rows), rows)
        for ahead in range(chips)
    ]
    total = None
    for ref in (own_ref, other_ref):
        q = jnp.concatenate([ref[0, here, place, :] for place in places], axis=0)
        part = lax.dot_general(
            q, ref[1, here], (((1,), (1,)), ((), ())), preferred_element_type=jnp.float32
        )
        total = part if total is None else total + part
    total = total * scale
    s_ref[:, here] = total.reshape(chips, rows, total.shape[1])


def mix_kernel(index_ref, table_ref, p_ref, v_ref, o_ref):
    seqs = o_ref.shape[0]
    size = v_ref.shape[2] // seqs
    _, chips, heads, rows, residues = p_ref.shape
    pairs = heads // 2
    step = pl.program_id(0)
    side = lax.div(step, pairs)
    first = 2 * lax.rem(step, pairs)
    start = lax.rem(index_ref[0] + side, 2) * heads + first
    mixed = []
    for head in range(2):
        probs = p_ref[side, :, first + head].reshape(chips * rows, residues)
        mixed.append(
            jnp.dot(probs, v_ref[start + head], preferred_element_type=jnp.float32).astype(
                jnp.bfloat16
            )
        )
    places = [
        pl.ds(pl.multiple_of(ring_place(index_ref, table_ref, ahead) * rows, rows), rows)
        for ahead in range(chips)
    ]
    for seq in range(seqs):
        joined = jnp.concatenate(
            [block[:, seq * size : (seq + 1) * size] for block in mixed], axis=1
        )
        for ahead, place in enumerate(places):
            o_ref[seq, place, :] = joined[ahead * rows : (ahead + 1) * rows]


def cost(flops, moved):
    return pl.CostEstimate(flops=int(flops), bytes_accessed=int(moved), transcendentals=0)


def projections(alignment, qkv_weight, index, depth_count, head_count):
    seqs, residues, features = alignment.shape
    heads = head_count // 2
    size = features // head_count
    rows = 256 if residues % 256 == 0 else residues
    cols = heads * size
    steps = residues // rows
    bf16 = jnp.bfloat16
    x_spec = pl.BlockSpec((seqs, rows, features), lambda i, *_: (0, i, 0))
    vmem = pl.BlockSpec(memory_space=pltpu.VMEM)
    qk_shape = jax.ShapeDtypeStruct((2, heads, residues, seqs * size), bf16)
    params = pltpu.CompilerParams(vmem_limit_bytes=48 << 20)

    def weight_specs(pick):
        return [
            pl.BlockSpec((features, cols), lambda i, index, _: (0, pick(lax.rem(index[0], 2)))),
            pl.BlockSpec((features, cols), lambda i, index, _: (0, 2 + pick(lax.rem(index[0], 2)))),
        ]

    flops = 4 * seqs * residues * features * cols
    moved = 2 * (seqs * residues * features + 2 * features * cols + 2 * seqs * residues * cols)
    normed, sent = pl.pallas_call(
        norm_send_kernel,
        out_shape=(jax.ShapeDtypeStruct(alignment.shape, bf16), qk_shape),
        grid_spec=pltpu.PrefetchScalarGridSpec(
            num_scalar_prefetch=2,
            grid=(steps,),
            in_specs=[x_spec] + weight_specs(lambda half: 1 - half),
            out_specs=[vmem, vmem],
        ),
        compiler_params=params,
        cost_estimate=cost(flops, moved + 2 * alignment.size),
        name="norm_send",
    )(index, depth_count, alignment, qkv_weight, qkv_weight)
    own = pl.pallas_call(
        functools.partial(own_kernel, residues),
        out_shape=qk_shape,
        grid_spec=pltpu.PrefetchScalarGridSpec(
            num_scalar_prefetch=2,
            grid=(1,),
            in_specs=[vmem] + weight_specs(lambda half: half),
            out_specs=vmem,
        ),
        compiler_params=params,
        cost_estimate=cost(flops, moved),
        name="own_project",
    )(index, depth_count, normed, qkv_weight, qkv_weight)
    return sent, own, normed


def value_projection(normed, qkv_weight, head_count):
    seqs, residues, features = normed.shape
    size = features // head_count
    rows = residues
    steps = residues // rows
    flops = 2 * seqs * residues * features * features
    moved = 2 * (2 * seqs * residues * features + features * features)
    bf16 = jnp.bfloat16
    params = pltpu.CompilerParams(vmem_limit_bytes=48 << 20)
    return pl.pallas_call(
        functools.partial(value_kernel, rows),
        out_shape=jax.ShapeDtypeStruct((head_count, residues, seqs * size), bf16),
        grid=(steps,),
        in_specs=[
            pl.BlockSpec(memory_space=pltpu.VMEM),
            pl.BlockSpec((features, features), lambda i: (0, 2)),
        ],
        out_specs=pl.BlockSpec(memory_space=pltpu.VMEM),
        compiler_params=params,
        cost_estimate=cost(flops, moved),
        name="value_project",
    )(normed, qkv_weight)


def scores_of(own, other, index, table, depth_count, size):
    _, heads, residues, inner = own.shape
    chips = table.shape[0] // 2
    rows = residues // chips
    spec = pl.BlockSpec(memory_space=pltpu.VMEM)
    return pl.pallas_call(
        functools.partial(score_kernel, size),
        out_shape=jax.ShapeDtypeStruct((chips, heads, rows, residues), jnp.float32),
        grid_spec=pltpu.PrefetchScalarGridSpec(
            num_scalar_prefetch=3,
            grid=(heads,),
            in_specs=[spec, spec],
            out_specs=spec,
        ),
        compiler_params=pltpu.CompilerParams(vmem_limit_bytes=32 << 20),
        cost_estimate=cost(4 * heads * residues * residues * inner, 4 * own.size + 4 * heads * residues**2),
        name="scores",
    )(index, table, depth_count, own, other)


def row_mix_of(probs, values, index, table, seqs, head_count):
    _, chips, heads, rows, residues = probs.shape
    inner = values.shape[2]
    size = inner // seqs
    pairs = heads // 2

    def pair_at(g, index):
        core = lax.rem(index[0] + lax.div(g, pairs), 2)
        return core * pairs + lax.rem(g, pairs)

    return pl.pallas_call(
        mix_kernel,
        out_shape=jax.ShapeDtypeStruct((seqs, residues, head_count * size), jnp.bfloat16),
        grid_spec=pltpu.PrefetchScalarGridSpec(
            num_scalar_prefetch=2,
            grid=(2 * pairs,),
            in_specs=[pl.BlockSpec(memory_space=pltpu.VMEM)] * 2,
            out_specs=pl.BlockSpec(
                (seqs, residues, 2 * size), lambda g, index, _: (0, 0, pair_at(g, index))
            ),
        ),
        compiler_params=pltpu.CompilerParams(vmem_limit_bytes=32 << 20),
        cost_estimate=cost(2 * probs.size * inner, 2 * (probs.size + 2 * values.size)),
        name="row_mix",
    )(index, table, probs, values)


class Links:
    def __init__(self):
        self.devices = lax.axis_size("seq")
        self.chips = self.devices // 2
        self.ring = ring_of(self.chips)
        places = [self.ring.index(chip) for chip in range(self.chips)]
        self.table = jnp.asarray(places + self.ring, jnp.int32)
        self.index = lax.axis_index("seq").astype(jnp.int32).reshape(1)

    def send(self, value, ahead):
        pairs = []
        for place, chip in enumerate(self.ring):
            target = self.ring[(place + ahead) % self.chips]
            pairs += [(2 * chip + core, 2 * target + core) for core in range(2)]
        return lax.ppermute(value, "seq", pairs)

    def swap(self, value):
        return lax.ppermute(value, "seq", [(i, i ^ 1) for i in range(self.devices)])


def reduce_scatter(links, scores):
    chips, _, rows, _ = scores.shape
    half = rows // 2
    low, high = slice(0, half), slice(half, rows)
    deep = chips // 2
    chains = [[(1, low), (-1, high)], [(1, high), (-1, low)]]

    def share(way, part, far):
        return scores[way * far % chips, :, part]

    moving = [None, None]
    gate = None
    for far in range(deep, 0, -1):
        for group in range(2):
            if group == 1 and far == deep:
                continue
            chain = chains[group]
            if moving[group] is None:
                sums = [share(way, part, far).astype(jnp.float16) for way, part in chain]
            else:
                arrived, _ = lax.optimization_barrier((moving[group], gate))
                sums = [
                    (value.astype(jnp.float32) + share(way, part, far)).astype(jnp.float16)
                    for value, (way, part) in zip(arrived, chain)
                ]
            gate = sums
            moving[group] = [links.send(value, way) for value, (way, _) in zip(sums, chain)]

    def settle(part, *arrived):
        total = scores[0, :, part]
        for value in arrived:
            total = total + value.astype(jnp.float32)
        return total

    (low_ahead, high_back), (high_ahead, low_back) = moving
    parts = [settle(low, low_ahead, low_back), settle(high, high_ahead, high_back)]
    return jnp.concatenate(parts, axis=1)


def all_gather(links, own, side):
    chips = links.chips
    heads, rows, width = own.shape
    half = rows // 2
    deep = chips // 2
    gathered = jnp.zeros((2, chips) + own.shape, own.dtype)
    side = list(side)
    done = []
    batches = [(0, own)]
    ahead = back = own
    for far in range(1, deep):
        ahead = links.send(ahead, 1)
        back = links.send(back, -1)
        batches += [(chips - far, ahead), (far, back)]
        if side:
            (ahead, back), kept = lax.optimization_barrier(((ahead, back), side.pop(0)))
            done.append(kept)
    batches.append((deep, [links.send(ahead[:, :half], 1), links.send(back[:, half:], -1)]))
    for far, batch in batches:
        piece = jnp.concatenate(batch, axis=1) if far == deep else batch
        for core, value in enumerate((piece, links.swap(piece))):
            gathered = lax.dynamic_update_slice(gathered, value[None, None], (core, far, 0, 0, 0))
    return gathered, done + side


ROWS = 4
REACH = {1: (0, 1, 2, 3, 4, -1), 2: (0, 1, 2, 3, -2, -1, 4, 5)}


def taps_kernel(w_ref, near_ref, far_ref):
    size = w_ref.shape[1]
    zero = jnp.zeros((size, size), w_ref.dtype)
    for dilation, out_ref in ((1, near_ref), (2, far_ref)):
        for which in range(2):
            base = 9 * (2 * (dilation - 1) + which)
            for col in range(3):
                for slot, row in enumerate(REACH[dilation]):
                    pieces = []
                    for out_row in range(ROWS):
                        step, rest = divmod(row - out_row, dilation)
                        live = rest == 0 and -1 <= step <= 1
                        pieces.append(w_ref[base + 3 * (step + 1) + col] if live else zero)
                    out_ref[which, col, slot * size : (slot + 1) * size, :] = jnp.concatenate(
                        pieces, axis=1
                    )


def contact_kernel(
    index_ref, pf_ref, pair_ref, near_ref, far_ref, head_ref, o_ref, u_ref, v_ref, hid_ref
):
    blocks, _, residues = pf_ref.shape
    lanes = pair_ref.shape[1]
    size = lanes // ROWS
    half = lanes // 2
    bf16 = jnp.bfloat16
    position = lax.broadcasted_iota(jnp.int32, (residues, lanes), 0)
    lane_row = lax.broadcasted_iota(jnp.int32, (1, lanes), 1) // size

    def masked(m, values):
        if 2 <= m < blocks - 2:
            return values
        row = index_ref[0] * o_ref.shape[0] + ROWS * (m - 2) + lane_row
        return jnp.where((row >= 0) & (row < residues), values, 0.0)

    def spread(ref, m, values, dilation):
        ref[1, m] = values.astype(bf16)
        left = jnp.where(position >= dilation, pltpu.roll(values, dilation, 0), 0.0)
        ref[0, m] = left.astype(bf16)
        right = jnp.where(
            position < residues - dilation, pltpu.roll(values, residues - dilation, 0), 0.0
        )
        ref[2, m] = right.astype(bf16)

    def conv(ref, m, w_ref, which, dilation):
        before = max(m - 1, 0)
        after = min(m + 1, blocks - 1)
        windows = []
        for col in range(3):
            low = ref[col, before, :, half:]
            high = ref[col, after, :, :half]
            if dilation == 1:
                lane = lax.broadcasted_iota(jnp.int32, low.shape, 1)
                edge = [jnp.where(lane < size, high, low)]
            else:
                edge = [low, high]
            windows += [ref[col, m]] + edge
        window = jnp.concatenate(windows, axis=1)
        weight = w_ref[which].reshape(window.shape[1], lanes)
        return jnp.dot(window, weight, preferred_element_type=jnp.float32)

    def start(m):
        hidden = lax.dot_general(
            pf_ref[m], pair_ref[...], (((0,), (0,)), ((), ())), preferred_element_type=jnp.float32
        )
        hid_ref[m] = hidden
        spread(u_ref, m, hidden, 1)

    for m in range(blocks):
        start(m)

    def first(m):
        inner = masked(m, jnp.maximum(conv(u_ref, m, near_ref, 0, 1), 0.0))
        spread(v_ref, m, inner, 1)

    for m in range(blocks):
        first(m)

    def second(m):
        hidden = masked(m, hid_ref[m] + conv(v_ref, m, near_ref, 1, 1))
        hid_ref[m] = hidden
        spread(u_ref, m, hidden, 2)

    for m in range(1, blocks - 1):
        second(m)

    def third(m):
        inner = masked(m, jnp.maximum(conv(u_ref, m, far_ref, 0, 2), 0.0))
        spread(v_ref, m, inner, 2)

    for m in range(1, blocks - 1):
        third(m)

    group = lax.broadcasted_iota(jnp.int32, (lanes, 128), 0) // size
    slot = lax.broadcasted_iota(jnp.int32, (lanes, 128), 1)

    def last(m, logits):
        hidden = hid_ref[m] + conv(v_ref, m, far_ref, 1, 2)
        weighed = hidden * head_ref[...]
        picks = jnp.where(slot == ROWS * (m - 2) + group, 1.0, 0.0).astype(bf16)
        for _ in range(3):
            coarse = weighed.astype(bf16)
            logits = logits + jnp.dot(coarse, picks, preferred_element_type=jnp.float32)
            weighed = weighed - coarse.astype(jnp.float32)
        return logits

    logits = jnp.zeros((residues, 128), jnp.float32)
    for m in range(2, blocks - 2):
        logits = last(m, logits)
    o_ref[...] = 1.0 / (1.0 + jnp.exp(-logits.T[: o_ref.shape[0]]))


def spread_taps(conv_weight):
    kinds, taps, size, _ = conv_weight.shape
    flipped = conv_weight.transpose(0, 1, 3, 2).reshape(kinds * taps, size, size)
    return pl.pallas_call(
        taps_kernel,
        out_shape=tuple(
            jax.ShapeDtypeStruct((2, 3, len(REACH[d]) * size, ROWS * size), conv_weight.dtype)
            for d in (1, 2)
        ),
        cost_estimate=cost(0, 6 << 20),
        name="spread_taps",
    )(flipped)


def window_kernel(index_ref, table_ref, p_ref, pf_ref, cols_ref, rows_ref):
    cores, chips, heads, rows, residues = p_ref.shape
    blocks, taken, _ = pf_ref.shape
    band = ROWS * blocks
    own_rows = band - 4 * ROWS
    first = index_ref[0] * own_rows - 2 * ROWS
    wide = cols_ref.shape[1] // (cores * heads)
    tall = rows_ref.shape[0] // (cores * heads)
    left = jnp.clip(lax.div(first, 128) * 128, 0, residues - wide)
    top = jnp.clip(lax.div(first, rows) * rows, 0, residues - tall)
    core = lax.rem(index_ref[0], 2)
    place = table_ref[lax.div(index_ref[0], 2)]
    lanes = pl.ds(pl.multiple_of(left, 128), wide)
    for ahead in range(chips):
        chip = ring_place(index_ref, table_ref, ahead)
        there = pl.ds(pl.multiple_of(chip * rows, rows), rows)
        for side in range(cores):
            for head in range(heads):
                slot = side * heads + head
                cols_ref[there, slot * wide : (slot + 1) * wide] = p_ref[side, ahead, head, :, lanes]
    for step in range(tall // rows):
        ahead = lax.rem(table_ref[lax.div(top, rows) + step] - place + chips, chips)
        for side in range(cores):
            for head in range(heads):
                start = (side * heads + head) * tall + step * rows
                rows_ref[start : start + rows, :] = p_ref[side, ahead, head]

    def picks(extent, base, out_rows, start):
        count = cores * heads * extent
        at = lax.broadcasted_iota(jnp.int32, (1, count), 1)
        slot = lax.div(at, extent)
        side = lax.div(slot, heads)
        head = lax.rem(side + core, 2) * heads + slot - side * heads
        have = head * 2048 + base + at - slot * extent
        out = start + lax.broadcasted_iota(jnp.int32, (out_rows, 1), 0)
        block = lax.div(out, taken)
        rest = out - block * taken
        head = lax.div(rest, ROWS)
        row = first + ROWS * block + rest - head * ROWS
        want = jnp.where((row >= 0) & (row < residues), head * 2048 + row, -1)
        return jnp.where(want == have, 1.0, 0.0).astype(jnp.bfloat16)

    step = blocks
    for block in range(0, blocks, step):
        by_col = lax.dot_general(
            picks(wide, left, step * taken, block * taken),
            cols_ref[...],
            (((1,), (1,)), ((), ())),
            preferred_element_type=jnp.float32,
        )
        by_row = jnp.dot(
            picks(tall, top, step * taken, block * taken),
            rows_ref[...],
            preferred_element_type=jnp.float32,
        )
        both = ((by_col + by_row) * (residues * 0.5)).astype(jnp.bfloat16)
        pf_ref[block : block + step] = both.reshape(step, taken, residues)


def contact_head(links, probs, pair_weight, taps, head_weight):
    cores, chips, heads, rows, residues = probs.shape
    own_rows = residues // links.devices
    blocks = own_rows // ROWS + 4
    count = cores * heads
    wide = min(256, residues)
    tall = max(2 * rows, 64)
    smem = pl.BlockSpec(memory_space=pltpu.SMEM)
    vmem = pl.BlockSpec(memory_space=pltpu.VMEM)
    pair_features = pl.pallas_call(
        window_kernel,
        out_shape=jax.ShapeDtypeStruct((blocks, ROWS * count, residues), jnp.bfloat16),
        in_specs=[smem, smem, vmem],
        out_specs=vmem,
        scratch_shapes=[
            pltpu.VMEM((residues, count * wide), jnp.bfloat16),
            pltpu.VMEM((count * tall, residues), jnp.bfloat16),
        ],
        compiler_params=pltpu.CompilerParams(vmem_limit_bytes=40 << 20),
        cost_estimate=cost(2 * blocks * ROWS * count**2 * residues * (wide + tall), 2 * probs.size),
        name="pair_window",
    )(links.index, links.table, probs)
    return contact_call(links.index, pair_features, pair_weight, taps, head_weight, own_rows)


def contact_call(index, pair_features, pair_weight, taps, head_weight, own_rows):
    blocks, _, residues = pair_features.shape
    channels = pair_weight.shape[0]
    same = jnp.eye(ROWS, dtype=pair_weight.dtype)
    pair = (pair_weight.T[:, None, None, :] * same[None, :, :, None]).reshape(-1, ROWS * channels)
    head = jnp.tile(head_weight, ROWS)[None]
    lanes = ROWS * channels
    vmem = pl.BlockSpec(memory_space=pltpu.VMEM)
    work = 2 * residues * lanes * lanes * (13 * blocks + 17 * (blocks - 2))
    return pl.pallas_call(
        contact_kernel,
        out_shape=jax.ShapeDtypeStruct((own_rows, residues), jnp.float32),
        in_specs=[pl.BlockSpec(memory_space=pltpu.SMEM)] + [vmem] * 5,
        out_specs=vmem,
        scratch_shapes=[
            pltpu.VMEM((3, blocks, residues, lanes), jnp.bfloat16),
            pltpu.VMEM((3, blocks, residues, lanes), jnp.bfloat16),
            pltpu.VMEM((blocks, residues, lanes), jnp.float32),
        ],
        compiler_params=pltpu.CompilerParams(vmem_limit_bytes=48 << 20),
        cost_estimate=cost(work // 4, 4 << 20),
        name="contact_head",
    )(index, pair_features, pair, taps[0], taps[1], head)


def local(alignment, depth_count, qkv_weight, pair_weight, conv_weight, head_weight):
    seqs, residues, features = alignment.shape
    head_count = pair_weight.shape[1]
    size = features // head_count
    links = Links()
    sent, own, normed = projections(alignment, qkv_weight, links.index, depth_count, head_count)
    other = links.swap(sent)
    scores = scores_of(own, other, links.index, links.table, depth_count, size)
    summed = reduce_scatter(links, scores)
    probabilities = jax.nn.softmax(summed * (1.0 / LINK_SCALE), axis=-1).astype(jnp.bfloat16)
    probabilities, normed, conv_weight = lax.optimization_barrier(
        (probabilities, normed, conv_weight)
    )
    values = value_projection(normed, qkv_weight, head_count)
    gathered, (values, taps) = all_gather(links, probabilities, (values, spread_taps(conv_weight)))
    row_mix = row_mix_of(gathered, values, links.index, links.table, seqs, head_count)
    contacts = contact_head(links, gathered, pair_weight, taps, head_weight)
    return (row_mix, contacts)


def solution(mesh):
    return jax.shard_map(
        local,
        mesh=mesh,
        in_specs=(P(("grp", "seq"), None, None), P("grp"), P(), P(), P(), P()),
        out_specs=(P(("grp", "seq"), None, None), P(("grp", "seq"), None)),
        check_vma=False,
    )
```
